32 devices in a mesh: orig: 8 (over z, core), dest: 4 (over y, x).
Axes of the slice: x: 2, y: 2, z: 4, core: 2. Of those that a mesh axis runs over, the one named last changes fastest.
Arguments:
- counts: int32 [192, 48, 1024], P('orig', None, 'dest'), may hold values from 0 to 96, as said below
- anchor_factor: float32 [192, 32], P('orig'), may hold values from 0.3 to 3
- dest_factor: float32 [1024, 32], P(('dest', 'orig')), may hold values from 0.3 to 3
- hour_factor: float32 [48, 32], replicated, may hold values from 0.3 to 3
- weights: float32 [32], replicated, may hold values from 0.06 to 0.5
Outputs:
- anchor_out: float32 [192, 32], P('orig')
- dest_out: float32 [1024, 32], P(('dest', 'orig'))
- hour_out: float32 [48, 32], replicated
- weights_out: float32 [32], replicated
The draws below stay inside these ranges and needn't reach their ends.
Inputs may be any that keep to these rules, and one draw needn't show every extreme that they name: `counts`: whole numbers of trips; many entries are zero.
All inputs are finite; a program needn't handle non-finite values.
Results may differ from the reference program's by a relative error of at most 0.00015.
Values sent between devices are 32-bit elements; how exact they have to be, the bound alone decides.
A program may use at most 64 MiB of HBM per device.

```python
import math
import jax
import jax.numpy as jnp
from jax import lax

I_DEV = 24
K = 48
R = 32
INNER = 2
OUTER = 2
NI = 192
NJ = 1024
N_ORIG = 8


def draw_counts(key, part):
    subkeys = jax.random.split(jax.random.fold_in(key, 11), 4)
    anchor_exp = jax.random.randint(subkeys[0], (NI, 4), 0, 5, dtype=jnp.int32)
    hour_exp = jax.random.randint(subkeys[1], (K, 4), 0, 4, dtype=jnp.int32)
    dest_exp = jax.random.randint(subkeys[2], (NJ, 4), 0, 6, dtype=jnp.int32)
    anchor_level = jnp.left_shift(jnp.ones((NI, 4), jnp.int32), anchor_exp)
    hour_level = jnp.left_shift(jnp.ones((K, 4), jnp.int32), hour_exp)
    dest_level = jnp.left_shift(jnp.ones((NJ, 4), jnp.int32), dest_exp)
    total = jnp.zeros((NI, K, NJ), jnp.int32)
    for term in range(4):
        total = total + anchor_level[:, term][:, None, None] * hour_level[:, term][None, :, None] * dest_level[:, term][None, None, :]
    noise = jax.random.randint(subkeys[3], (NI, K, NJ), 0, 4, dtype=jnp.int32)
    return jnp.minimum(total * noise // 128, 96).astype(jnp.int32)


def block_scale(rng, dims, shards, least, high):
    factor_of, own = 1.0, jax.random.fold_in(rng, 6)
    for dim, shards_of in shards:
        draws = jnp.exp(jax.random.uniform(jax.random.fold_in(own, dim), (shards_of,), jnp.float32, least / len(shards), high / len(shards)))
        factor_of = factor_of * jnp.repeat(draws, dims[dim] // shards_of).reshape([-1 if axis == dim else 1 for axis in range(len(dims))])
    return factor_of


def setup_inputs(seed: int = 0) -> dict:
    key_list = jax.random.split(jax.random.key(seed), 6)
    return {
        "counts": draw_counts(jax.random.fold_in(key_list[5], 71), 0),
        "anchor_factor": jnp.clip(jnp.exp(math.log(3.0) - 2.3025851 * jax.random.uniform(key_list[1], (NI, R), jnp.float32) ** block_scale(key_list[1], (NI, R), ((0, 8),), -0.2, 0.2)), 0.3, 3.0),
        "dest_factor": jnp.clip(jnp.exp(math.log(3.0) - 2.3025851 * jax.random.uniform(key_list[2], (NJ, R), jnp.float32) ** block_scale(key_list[2], (NJ, R), ((0, 32),), -0.2, 0.2)), 0.3, 3.0),
        "hour_factor": jnp.clip(jnp.exp(jax.random.uniform(key_list[3], (K, R), jnp.float32, math.log(0.3), math.log(3.0))), 0.3, 3.0),
        "weights": jnp.clip(jnp.exp(jax.random.uniform(key_list[4], (R,), jnp.float32, math.log(0.06), math.log(0.5))), 0.06, 0.5),
    }


HIGH = lax.Precision.HIGHEST


def contract(counts, p_fac, q_fac, s_fac):
    blocks = counts.reshape(N_ORIG, I_DEV, K, NJ)
    p_blocks = p_fac.reshape(N_ORIG, I_DEV, R)

    def step(carry, item):
        block, p_part = item
        values = block.astype(jnp.float32).reshape(I_DEV * K, NJ)
        khatri = (p_part[:, None, :] * q_fac[None, :, :]).reshape(I_DEV * K, R)
        model = lax.dot_general(khatri, s_fac, (((1,), (1,)), ((), ())), precision=HIGH)
        ratio = values / model
        along = jnp.dot(ratio, s_fac, precision=HIGH).reshape(I_DEV, K, R)
        phi_i = jnp.sum(along * q_fac[None, :, :], axis=1)
        phi_k = jnp.sum(along * p_part[:, None, :], axis=0)
        phi_j = lax.dot_general(ratio, khatri, (((0,), (0,)), ((), ())), precision=HIGH)
        return (carry[0] + phi_k, carry[1] + phi_j), phi_i

    init = (jnp.zeros((K, R), jnp.float32), jnp.zeros((NJ, R), jnp.float32))
    (phi_k, phi_j), phi_i = lax.scan(step, init, (blocks, p_blocks))
    return phi_i.reshape(NI, R), phi_k, phi_j


def reference(counts, anchor_factor, dest_factor, hour_factor, weights):
    anchor, dest, hour, weight = anchor_factor, dest_factor, hour_factor, weights
    for outer in range(OUTER):
        growth = anchor * weight[None, :]
        for inner in range(INNER):
            phi_i, phi_k, phi_j = contract(counts, growth, hour, dest)
            growth = growth * (phi_i / (K * NJ))
        weight = jnp.sum(growth, axis=0) / NI
        anchor = growth / weight[None, :]
        growth = dest * weight[None, :]
        for inner in range(INNER):
            phi_i, phi_k, phi_j = contract(counts, anchor, hour, growth)
            growth = growth * (phi_j / (NI * K))
        weight = jnp.sum(growth, axis=0) / NJ
        dest = growth / weight[None, :]
        growth = hour * weight[None, :]
        for inner in range(INNER):
            phi_i, phi_k, phi_j = contract(counts, anchor, growth, dest)
            growth = growth * (phi_k / (NI * NJ))
        weight = jnp.sum(growth, axis=0) / K
        hour = growth / weight[None, :]
    return anchor, dest, hour, weight
```

```python
import functools

import jax
import jax.numpy as jnp
from jax import lax
from jax.experimental import pallas as pl
from jax.experimental.pallas import tpu as pltpu
from jax.sharding import PartitionSpec as P

INNER = 2
OUTER = 2
LANES = 128
F32 = jnp.float32
BF16 = jnp.bfloat16
HIGH = lax.Precision.HIGHEST
MESH = pl.DeviceIdType.MESH


def iota(shape, dim):
    return lax.broadcasted_iota(jnp.int32, shape, dim)


def kernel(nz, ndest, counts_in, anchor_in, dest_in, hour_in, weight_in,
           anchor_out, dest_out, hour_out, weight_out,
           cnts, ucur, ccur, chour, tcur, bmod, balo, khbuf,
           ubuf, zbuf, hbuf, gbuf, abuf, tbuf, cbuf, dbuf, anchor_ref, hour_ref, weight_ref,
           u_send, u_recv, z_send, z_recv, h_send, h_recv, g_send, g_recv, t_sem, c_sem, d_sem, a_sem, v_sem, in_sem):
    _, nrow, nhour, ncol = cnts.shape
    rank = hour_ref.shape[0]
    piece = dbuf.shape[1]
    copies = LANES // rank
    half = ncol // 2
    khalf = nhour // 2
    nx = 2 * ndest
    norig = 2 * nz
    nchip = nz * ndest
    total_rows = nrow * norig
    total_cols = ncol * ndest
    me_orig = lax.axis_index("orig")
    me_dest = lax.axis_index("dest")
    zi = me_orig // 2
    core = me_orig % 2
    other = 1 - core
    xi = me_dest * 2 + core
    chip = zi * ndest + me_dest
    partner = {"orig": zi * 2 + other}
    chunks = nrow // 8

    xpeers = []
    for t in range(1, nx):
        idx = (xi + t) % nx
        xpeers.append({"orig": zi * 2 + idx % 2, "dest": idx // 2})
    zpeers = [{"orig": (zi + t) % nz * 2 + core} for t in range(1, nz)]
    opeers = [{"orig": (me_orig + t) % norig} for t in range(1, norig)]
    cpeers, dpeers = [], []
    for t in range(nchip):
        idx = (chip + t) % nchip
        z, d = idx // ndest, idx % ndest
        if t:
            cpeers.append({"orig": z * 2 + core, "dest": d})
        dpeers.append({"orig": z * 2 + other, "dest": d})

    small = [pltpu.make_async_copy(a, b, in_sem.at[q]) for q, (a, b) in enumerate(
        ((anchor_in, anchor_ref), (dest_in, dbuf.at[me_orig]), (hour_in, hour_ref), (weight_in, weight_ref)))]
    large = [pltpu.make_async_copy(counts_in.at[pl.ds(8 * s, 8)], cnts.at[core, pl.ds(8 * s, 8)], in_sem.at[4 + s])
             for s in range(chunks)]
    for dma in small + large:
        dma.start()
    barrier = pltpu.get_barrier_semaphore()
    for who in cpeers + dpeers:
        pl.semaphore_signal(barrier, inc=1, device_id=who, device_id_type=MESH)

    def remote(src, dst, send, recv, who):
        return pltpu.make_async_remote_copy(
            src_ref=src, dst_ref=dst, send_sem=send, recv_sem=recv, device_id=who, device_id_type=MESH)

    def start(ref, send, recv, peers, me):
        for who in peers:
            remote(ref.at[me], ref.at[me], send, recv, who).start()

    def wait_bytes(ref, sem):
        pltpu.make_async_copy(ref, ref, sem).wait()

    def add_up(ref, slots):
        total = ref[slots[0]]
        for s in slots[1:]:
            total = total + ref[s]
        return total

    lane = iota((1, LANES), 1)
    group = lane // rank
    spread = (iota((rank, LANES), 1) % rank == iota((rank, LANES), 0)).astype(F32)
    diag = iota((rank, LANES), 1) == iota((rank, LANES), 0)
    diag_all = iota((rank, LANES), 1) % rank == iota((rank, LANES), 0)
    eye = (iota((rank, rank), 0) == iota((rank, rank), 1)).astype(F32)

    def to_column(row):
        return jnp.sum(jnp.where(diag, jnp.broadcast_to(row, (rank, LANES)), 0.0), axis=1, keepdims=True)

    def to_row(column):
        return jnp.sum(jnp.where(diag_all, jnp.broadcast_to(column, (rank, LANES)), 0.0), axis=0, keepdims=True)

    def sum_groups(x):
        step = rank
        while step < LANES:
            x = x + pltpu.roll(x, step, 1)
            step *= 2
        return x

    def spread_group(x, b):
        return sum_groups(jnp.where(group == b, x, 0.0))

    def pair_up(x):
        return x + pltpu.roll(x, rank, 1)

    def twice(x):
        return jnp.concatenate([x, x], axis=1)

    hrow = gbuf.shape[2]
    hblocks = khalf // hrow

    def pack_hour(p, extra):
        out = jnp.broadcast_to(extra, (hrow, LANES))
        for b in range(hblocks):
            out = jnp.where(group == b, p[b * hrow:(b + 1) * hrow], out)
        return out

    def unpack_hour(s):
        return jnp.concatenate([spread_group(s, b) for b in range(hblocks)], axis=0)

    for dma in (small[0], small[2], small[3]):
        dma.wait()
    own_anchor = lax.dot(anchor_ref[...], spread, precision=HIGH)
    weight_row = jnp.sum(jnp.where(
        diag_all, jnp.broadcast_to(to_rows(weight_ref[...], rank), (rank, LANES)), 0.0), axis=0, keepdims=True)
    abuf[core] = own_anchor * weight_row
    ccur[...] = lax.dot_general(hour_ref[...], spread, (((0,), (0,)), ((), ())), precision=HIGH)
    bmod[...] = jnp.zeros_like(bmod)
    balo[...] = jnp.zeros_like(balo)

    pl.semaphore_wait(barrier, 2 * nchip - 1)

    for who in opeers:
        remote(dest_in, dbuf.at[me_orig], d_sem.at[0], d_sem.at[1], who).start()

    def acopy(slot):
        return remote(abuf.at[slot], abuf.at[slot], a_sem.at[0], a_sem.at[1], partner)

    def vcopy(slot):
        return remote(counts_in, cnts.at[slot], v_sem.at[0], v_sem.at[1], partner)

    acopy(core).start()
    vcopy(core).start()

    def set_right(t, g):
        hi = t.astype(BF16).astype(F32)
        lo = t - hi
        model = jnp.concatenate([hi] * (copies // 2) + [lo] * (copies // 2), axis=0).astype(BF16)
        along = jnp.concatenate([hi, lo], axis=0).astype(BF16)
        for q in range(2):
            lanes = slice(q * LANES, (q + 1) * LANES)
            bmod[g, lanes, lanes] = model
            for part in range(2):
                balo[g, q * 2 * rank:(q + 1) * 2 * rank, (2 * part + q) * LANES:(2 * part + q + 1) * LANES] = along

    high_lane = (iota((1, 2 * LANES), 1) // rank) % 2 == 0

    def split_kh(left, right):
        kh = (left[:, None, :] * right[None, :, :]).reshape(left.shape[0] * right.shape[0], 2 * LANES)
        hi = kh.astype(BF16).astype(F32)
        return jnp.where(high_lane, hi, kh - hi).astype(BF16)

    def ratio_of(khs, values, g):
        model = jnp.dot(khs, bmod[g], preferred_element_type=F32)
        ratio = values / model
        rh = ratio.astype(BF16)
        rl = (ratio - rh.astype(F32)).astype(BF16)
        return rh, rl

    def along_of(rh, rl, g):
        return lax.dot_general(jnp.concatenate([rh, rl], axis=1), balo[g], (((1,), (1,)), ((), ())),
                               preferred_element_type=F32)

    def block(q, rows, hours, g):
        v = cnts[q, rows, hours, pl.ds(pl.multiple_of(g * half, half), half)]
        return v.reshape(-1, half).astype(F32)

    def anchor_step(e, before):
        left_right = jnp.concatenate([ccur[:khalf], ccur[khalf:]], axis=1)
        mixed = jnp.where(group < 2, ccur[:khalf], ccur[khalf:])
        for s in range(chunks):
            before(s)
            left = ucur[core, 8 * s:8 * s + 8]
            khs = split_kh(twice(left), left_right)
            along = None
            for g in range(2):
                values = jnp.concatenate([
                    block(core, slice(8 * s, 8 * s + 8), slice(q * khalf, (q + 1) * khalf), g)
                    for q in range(2)], axis=1)
                rh, rl = ratio_of(khs, values, g)
                part = along_of(rh, rl, g)
                along = part if along is None else along + part
            p = sum_groups(jnp.sum(along.reshape(8, khalf, LANES) * mixed[None, :, :], axis=1))
            ub = ubuf.at[e * chunks + s]
            ub[xi] = p
            start(ub, u_send.at[e * chunks + s], u_recv.at[e * chunks + s], xpeers, xi)

    def anchor_update(e):
        def update(s):
            ub = ubuf.at[e * chunks + s]
            wait_bytes(ub.at[pl.ds(0, nx - 1)], u_recv.at[e * chunks + s])
            rows = slice(8 * s, 8 * s + 8)
            for q in range(2):
                p = add_up(ub, range(q, nx, 2))
                ucur[q, rows] = ucur[q, rows] * (p / (nhour * total_cols))
        return update

    def both(s):
        rows = slice(8 * s, 8 * s + 8)
        return jnp.concatenate([ucur[0, rows], ucur[1, rows]], axis=1)

    def dest_phi(before, inner):
        dims = (((0,), (0,)), ((), ()))
        crow = 8 * nhour
        right = twice(ccur[...])
        total = None
        for s in range(chunks):
            before(s)
            if inner == 0:
                khs = split_kh(both(s), right)
                khbuf[s * crow:(s + 1) * crow] = khs
            else:
                khs = khbuf[s * crow:(s + 1) * crow]
            values = jnp.concatenate([
                block(q, slice(8 * s, 8 * s + 8), slice(None), core) for q in range(2)], axis=1)
            for g, r in enumerate(ratio_of(khs, values, core)):
                for q in range(2):
                    lanes = slice(q * LANES, (q + 1) * LANES)
                    part = lax.dot_general(khs[:, lanes], r[:, lanes], dims, preferred_element_type=F32)
                    total = part if total is None else total + part
        return total[:rank] + total[rank:2 * rank]

    hours = pl.ds(pl.multiple_of(core * khalf, khalf), khalf)

    def hour_phi(between):
        right = twice(chour[core])
        crow = 8 * khalf
        p = None
        for order, g in enumerate((core, other)):
            if order:
                between()
            for s in range(chunks):
                left = both(s)
                if order == 0:
                    khs = split_kh(left, right)
                    khbuf[s * crow:(s + 1) * crow] = khs
                else:
                    khs = khbuf[s * crow:(s + 1) * crow]
                values = jnp.concatenate([
                    block(q, slice(8 * s, 8 * s + 8), hours, g) for q in range(2)], axis=1)
                rh, rl = ratio_of(khs, values, g)
                mixed = jnp.where(group < 2, left[:, :LANES], left[:, LANES:])
                part = jnp.sum(along_of(rh, rl, g).reshape(8, khalf, LANES) * mixed[:, None, :], axis=0)
                p = part if p is None else p + part
        return sum_groups(p)

    small[1].wait()
    wait_bytes(dbuf.at[pl.ds(0, norig - 1)], d_sem.at[1])
    tall = lax.dot_general(eye, dbuf[...].reshape(ncol, rank), (((1,), (1,)), ((), ())), precision=HIGH)
    for g in range(2):
        tcur[g] = tall[:, g * half:(g + 1) * half]
        set_right(tall[:, g * half:(g + 1) * half], g)
    for dma in large:
        dma.wait()
    ucur[core] = abuf[core]
    acopy(other).wait_recv()
    ucur[other] = abuf[other]

    @pl.loop(0, OUTER)
    def _(outer):
        before = lambda s: None
        for inner in range(INNER):
            anchor_step(outer * INNER + inner, before)
            before = anchor_update(outer * INNER + inner)

        @pl.when(outer == 0)
        def _():
            vcopy(other).wait_recv()

        anchor_w = None
        for inner in range(INNER):
            e = outer * 2 + inner
            zb, zs, zr = zbuf.at[e], z_send.at[e], z_recv.at[e]
            p = dest_phi(before, inner)
            before = lambda s: None
            col = jnp.sum(ucur[0] + ucur[1], axis=0, keepdims=True)
            zb[zi] = jnp.concatenate([p, jnp.broadcast_to(col, (8, LANES))], axis=0)
            start(zb, zs, zr, zpeers, zi)
            wait_bytes(zb.at[pl.ds(0, nz - 1)], zr)
            s = add_up(zb, range(nz))
            growth = tcur[core] * (s[:rank] / (total_rows * nhour))
            if inner == 0:
                anchor_w = s[rank:rank + 1] / total_rows
                growth = growth / to_column(anchor_w)
            else:
                tbuf[outer, core] = growth
                remote(tbuf.at[outer, core], tbuf.at[outer, core], t_sem.at[0, outer], t_sem.at[1, outer],
                       partner).start()
            tcur[core] = growth
            set_right(growth, core)
        for q in range(2):
            ucur[q] = ucur[q] / anchor_w

        def far():
            remote(tbuf.at[outer, core], tbuf.at[outer, other], t_sem.at[0, outer], t_sem.at[1, outer],
                   partner).wait_recv()
            tcur[other] = tbuf[outer, other]
            set_right(tcur[other], other)

        for q in range(2):
            chour[q] = ccur[q * khalf:(q + 1) * khalf]
        pmine = hour_phi(far)
        dest_col = to_row(jnp.sum(tcur[0] + tcur[1], axis=1, keepdims=True))
        hb, hs, hr = hbuf.at[outer], h_send.at[outer], h_recv.at[outer]
        hb[chip] = pack_hour(pmine, dest_col)
        start(hb, hs, hr, cpeers, chip)
        wait_bytes(hb.at[pl.ds(0, nchip - 1)], hr)
        s = add_up(hb, range(nchip))
        dest_w = spread_group(s[:1], copies - 1) / (total_cols * nz)
        growth = chour[core] * (unpack_hour(s) / (total_rows * total_cols)) / dest_w
        chour[core] = growth
        cbuf[outer, core] = growth
        remote(cbuf.at[outer, core], cbuf.at[outer, core], c_sem.at[0, outer], c_sem.at[1, outer], partner).start()
        pmine = hour_phi(lambda: None)
        gb, gs, gr = gbuf.at[outer], g_send.at[outer], g_recv.at[outer]
        mine = core * nchip + chip
        gb[mine] = pack_hour(pmine, dest_col)
        for who in cpeers + dpeers:
            remote(gb.at[mine], gb.at[mine], gs, gr, who).start()
        remote(cbuf.at[outer, core], cbuf.at[outer, other], c_sem.at[0, outer], c_sem.at[1, outer],
               partner).wait_recv()
        chour[other] = cbuf[outer, other]
        wait_bytes(gb.at[pl.ds(0, 2 * nchip - 1)], gr)
        full = jnp.concatenate([
            chour[q] * (unpack_hour(add_up(gb, range(q * nchip, (q + 1) * nchip))) / (total_rows * total_cols))
            for q in range(2)], axis=0)
        w = jnp.sum(full, axis=0, keepdims=True) / nhour
        full = full / w
        ccur[...] = full

        @pl.when(outer == OUTER - 1)
        def _():
            anchor_out[...] = ucur[core][:, :rank]
            hour_out[...] = lax.dot_general(
                diag.astype(F32), ccur[...], (((1,), (1,)), ((), ())), precision=HIGH)
            weight_out[...] = w[:, :rank]
            place = (iota((piece, ncol), 1) == me_orig * piece + iota((piece, ncol), 0)).astype(F32)
            d = jnp.concatenate([tcur[0], tcur[1]], axis=1) / to_column(dest_w)
            dest_out[...] = lax.dot_general(place, d, (((1,), (1,)), ((), ())), precision=HIGH)

        @pl.when(outer < OUTER - 1)
        def _():
            for q in range(2):
                ucur[q] = ucur[q] * w
                tcur[q] = tcur[q] / to_column(dest_w)
                set_right(tcur[q], q)

    wait_bytes(dbuf.at[pl.ds(0, norig - 1)], d_sem.at[0])
    acopy(core).wait_send()
    vcopy(core).wait_send()
    for e in range(OUTER * INNER * chunks):
        wait_bytes(ubuf.at[e, pl.ds(0, nx - 1)], u_send.at[e])
    for e in range(OUTER * 2):
        wait_bytes(zbuf.at[e, pl.ds(0, nz - 1)], z_send.at[e])
    for e in range(OUTER):
        wait_bytes(tbuf.at[e, 0], t_sem.at[0, e])
        wait_bytes(cbuf.at[e, 0], c_sem.at[0, e])
        wait_bytes(hbuf.at[e, pl.ds(0, nchip - 1)], h_send.at[e])
        wait_bytes(gbuf.at[e, pl.ds(0, 2 * nchip - 1)], g_send.at[e])


def put_out(*refs):
    copies = [pltpu.make_async_copy(refs[q], refs[4 + q], refs[8].at[q]) for q in range(4)]
    for c in copies:
        c.start()
    for c in copies:
        c.wait()


def to_rows(row, rank):
    square = jnp.where(iota((rank, rank), 0) == iota((rank, rank), 1), jnp.broadcast_to(row, (rank, rank)), 0.0)
    return jnp.sum(square, axis=1, keepdims=True)


def on_device(counts, anchor_factor, dest_factor, hour_factor, weights):
    norig = lax.axis_size("orig")
    ndest = lax.axis_size("dest")
    nz, nx = norig // 2, 2 * ndest
    nchip = nz * ndest
    nrow, nhour, ncol = counts.shape
    rank = hour_factor.shape[1]
    khalf = nhour // 2
    chunks = nrow // 8
    hrow = -(-khalf // (8 * (LANES // rank - 1))) * 8
    dma = pltpu.SemaphoreType.DMA
    vmem = pltpu.VMEM
    outs = pl.pallas_call(
        functools.partial(kernel, nz, ndest),
        out_shape=[
            jax.ShapeDtypeStruct(anchor_factor.shape, F32),
            jax.ShapeDtypeStruct(dest_factor.shape, F32),
            jax.ShapeDtypeStruct((rank, nhour), F32),
            jax.ShapeDtypeStruct((1, rank), F32),
        ],
        in_specs=[pl.BlockSpec(memory_space=pltpu.HBM)] * 5,
        out_specs=[pl.BlockSpec(memory_space=pltpu.VMEM)] * 4,
        scratch_shapes=[
            vmem((2, nrow, nhour, ncol), counts.dtype),
            vmem((2, nrow, LANES), F32),
            vmem((nhour, LANES), F32),
            vmem((2, khalf, LANES), F32),
            vmem((2, rank, LANES), F32),
            vmem((2, 2 * LANES, 2 * LANES), BF16),
            vmem((2, 4 * rank, 4 * LANES), BF16),
            vmem((nrow * nhour, 2 * LANES), BF16),
            vmem((OUTER * INNER * chunks, nx, 8, LANES), F32),
            vmem((OUTER * 2, nz, rank + 8, LANES), F32),
            vmem((OUTER, nchip, hrow, LANES), F32),
            vmem((OUTER, 2 * nchip, hrow, LANES), F32),
            vmem((2, nrow, LANES), F32),
            vmem((OUTER, 2, rank, LANES), F32),
            vmem((OUTER, 2, khalf, LANES), F32),
            vmem((norig,) + dest_factor.shape, F32),
            vmem(anchor_factor.shape, F32),
            vmem((rank, nhour), F32),
            vmem((1, rank), F32),
            dma((OUTER * INNER * chunks,)), dma((OUTER * INNER * chunks,)),
            dma((OUTER * 2,)), dma((OUTER * 2,)),
            dma((OUTER,)), dma((OUTER,)),
            dma((OUTER,)), dma((OUTER,)),
            dma((2, OUTER)), dma((2, OUTER)), dma((2,)), dma((2,)), dma((2,)), dma((4 + chunks,)),
        ],
        compiler_params=pltpu.CompilerParams(
            collective_id=0, has_side_effects=True, vmem_limit_bytes=67043328),
    )(counts, anchor_factor, dest_factor, hour_factor.T, weights.reshape(1, rank))
    outs = pl.pallas_call(
        put_out,
        out_shape=[jax.ShapeDtypeStruct(o.shape, F32) for o in outs],
        in_specs=[pl.BlockSpec(memory_space=pltpu.VMEM)] * 4,
        out_specs=[pl.BlockSpec(memory_space=pltpu.HBM)] * 4,
        scratch_shapes=[dma((4,))],
    )(*outs)
    return outs[0], outs[1], outs[2].T, outs[3].reshape(rank)


def solution(mesh):
    return jax.shard_map(
        on_device,
        mesh=mesh,
        in_specs=(P("orig", None, "dest"), P("orig", None), P(("dest", "orig"), None), P(), P()),
        out_specs=(P("orig", None), P(("dest", "orig"), None), P(), P()),
        check_vma=False,
    )
```

```python
import functools

import jax
import jax.numpy as jnp
from jax import lax
from jax.experimental import pallas as pl
from jax.experimental.pallas import tpu as pltpu
from jax.sharding import PartitionSpec as P

INNER = 2
OUTER = 2
LANES = 128
F32 = jnp.float32
BF16 = jnp.bfloat16
HIGH = lax.Precision.HIGHEST
MESH = pl.DeviceIdType.MESH


def iota(shape, dim):
    return lax.broadcasted_iota(jnp.int32, shape, dim)


def kernel(nz, ndest, counts_in, anchor_in, dest_in, hour_in, weight_in,
           anchor_out, dest_out, hour_out, weight_out,
           cnts, ucur, ccur, chour, tcur, bmod, balo, khbuf,
           ubuf, zbuf, hbuf, gbuf, abuf, tbuf, cbuf, dbuf, anchor_ref, hour_ref, weight_ref,
           u_send, u_recv, z_send, z_recv, h_send, h_recv, g_send, g_recv, t_sem, c_sem, d_sem, a_sem, v_sem, in_sem):
    _, nrow, nhour, ncol = cnts.shape
    rank = hour_ref.shape[0]
    piece = dbuf.shape[1]
    copies = LANES // rank
    half = ncol // 2
    khalf = nhour // 2
    nx = 2 * ndest
    norig = 2 * nz
    nchip = nz * ndest
    total_rows = nrow * norig
    total_cols = ncol * ndest
    me_orig = lax.axis_index("orig")
    me_dest = lax.axis_index("dest")
    zi = me_orig // 2
    core = me_orig % 2
    other = 1 - core
    xi = me_dest * 2 + core
    chip = zi * ndest + me_dest
    partner = {"orig": zi * 2 + other}
    chunks = nrow // 8

    up = zi * 2 // nz
    own_place = (nz - 1 - zi) * (1 - up) + zi * up
    zline = []
    for t in range(nz - 1):
        place = t + (t - own_place + nz) // nz
        zline.append((nz - 1 - place) * (1 - up) + place * up)
    zline.append(zi)
    side = 1 - 2 * (me_dest % 2)
    if ndest == 4:
        plane = [3 - me_dest, me_dest + side, (me_dest + 2) % 4, me_dest]
    else:
        plane = [(me_dest + t) % ndest for t in range(1, ndest)] + [me_dest]
    xpeers = [{"orig": zi * 2 + c, "dest": d} for d in plane for c in (core, other)]
    xpeers = xpeers[:-2] + xpeers[-1:]
    zpeers = [{"orig": z * 2 + core} for z in zline[:-1]]
    opeers = [{"orig": z * 2 + c} for z in zline for c in (core, other)]
    opeers = opeers[:-2] + opeers[-1:]
    cpeers = [{"orig": z * 2 + core, "dest": d} for z in zline for d in plane][:-1]
    dpeers = [{"orig": z * 2 + other, "dest": d} for z in zline for d in plane]
    everyone = [who for pair in zip(cpeers, dpeers) for who in pair] + dpeers[-1:]

    small = [pltpu.make_async_copy(a, b, in_sem.at[q]) for q, (a, b) in enumerate(
        ((anchor_in, anchor_ref), (dest_in, dbuf.at[me_orig]), (hour_in, hour_ref), (weight_in, weight_ref)))]
    large = [pltpu.make_async_copy(counts_in.at[pl.ds(8 * s, 8)], cnts.at[core, pl.ds(8 * s, 8)], in_sem.at[4 + s])
             for s in range(chunks)]
    for dma in small + large:
        dma.start()
    barrier = pltpu.get_barrier_semaphore()
    near = opeers[:-1] + xpeers
    for who in near:
        pl.semaphore_signal(barrier, inc=1, device_id=who, device_id_type=MESH)

    def remote(src, dst, send, recv, who):
        return pltpu.make_async_remote_copy(
            src_ref=src, dst_ref=dst, send_sem=send, recv_sem=recv, device_id=who, device_id_type=MESH)

    def start(ref, send, recv, peers, me):
        for who in peers:
            remote(ref.at[me], ref.at[me], send, recv, who).start()

    def wait_bytes(ref, sem):
        pltpu.make_async_copy(ref, ref, sem).wait()

    def add_up(ref, slots):
        total = ref[slots[0]]
        for s in slots[1:]:
            total = total + ref[s]
        return total

    lane = iota((1, LANES), 1)
    group = lane // rank
    spread = (iota((rank, LANES), 1) % rank == iota((rank, LANES), 0)).astype(F32)
    diag = iota((rank, LANES), 1) == iota((rank, LANES), 0)
    diag_all = iota((rank, LANES), 1) % rank == iota((rank, LANES), 0)
    eye = (iota((rank, rank), 0) == iota((rank, rank), 1)).astype(F32)

    def to_column(row):
        return jnp.sum(jnp.where(diag, jnp.broadcast_to(row, (rank, LANES)), 0.0), axis=1, keepdims=True)

    def to_row(column):
        return jnp.sum(jnp.where(diag_all, jnp.broadcast_to(column, (rank, LANES)), 0.0), axis=0, keepdims=True)

    def sum_groups(x):
        step = rank
        while step < LANES:
            x = x + pltpu.roll(x, step, 1)
            step *= 2
        return x

    def spread_group(x, b):
        return sum_groups(jnp.where(group == b, x, 0.0))

    def pair_up(x):
        return x + pltpu.roll(x, rank, 1)

    def twice(x):
        return jnp.concatenate([x, x], axis=1)

    hrow = hbuf.shape[2]
    prow = gbuf.shape[2]
    hblocks = khalf // hrow

    def pack_hour(p, extra):
        out = jnp.broadcast_to(extra, (hrow, LANES))
        for b in range(hblocks):
            out = jnp.where(group == b, p[b * hrow:(b + 1) * hrow], out)
        return out

    def unpack_hour(s):
        return jnp.concatenate([spread_group(s, b) for b in range(hblocks)], axis=0)

    def unpack_tight(s):
        return jnp.concatenate([spread_group(s, b) for b in range(copies)], axis=0)

    for dma in (small[0], small[2], small[3]):
        dma.wait()
    own_anchor = lax.dot(anchor_ref[...], spread, precision=HIGH)
    weight_row = jnp.sum(jnp.where(
        diag_all, jnp.broadcast_to(to_rows(weight_ref[...], rank), (rank, LANES)), 0.0), axis=0, keepdims=True)
    abuf[core] = own_anchor * weight_row
    ccur[...] = lax.dot_general(hour_ref[...], spread, (((0,), (0,)), ((), ())), precision=HIGH)
    bmod[...] = jnp.zeros_like(bmod)
    balo[...] = jnp.zeros_like(balo)

    pl.semaphore_wait(barrier, len(near))

    for who in opeers:
        remote(dest_in, dbuf.at[me_orig], d_sem.at[0], d_sem.at[1], who).start()

    def acopy(slot):
        return remote(abuf.at[slot], abuf.at[slot], a_sem.at[0], a_sem.at[1], partner)

    def vcopy(slot):
        return remote(counts_in, cnts.at[slot], v_sem.at[0], v_sem.at[1], partner)

    acopy(core).start()
    vcopy(core).start()

    def set_right(t, g):
        hi = t.astype(BF16).astype(F32)
        lo = t - hi
        model = jnp.concatenate([hi] * (copies // 2) + [lo] * (copies // 2), axis=0).astype(BF16)
        along = jnp.concatenate([hi, lo], axis=0).astype(BF16)
        for q in range(2):
            lanes = slice(q * LANES, (q + 1) * LANES)
            bmod[g, lanes, lanes] = model
            for part in range(2):
                balo[g, q * 2 * rank:(q + 1) * 2 * rank, (2 * part + q) * LANES:(2 * part + q + 1) * LANES] = along

    high_lane = (iota((1, 2 * LANES), 1) // rank) % 2 == 0

    def split_kh(left, right):
        kh = (left[:, None, :] * right[None, :, :]).reshape(left.shape[0] * right.shape[0], 2 * LANES)
        hi = kh.astype(BF16).astype(F32)
        return jnp.where(high_lane, hi, kh - hi).astype(BF16)

    def ratio_of(khs, values, g):
        model = jnp.dot(khs, bmod[g], preferred_element_type=F32)
        ratio = values / model
        return ratio.astype(BF16), None

    def along_of(rh, rl, g):
        return lax.dot_general(rh, balo[g, :, :2 * LANES], (((1,), (1,)), ((), ())),
                               preferred_element_type=F32)

    def block(q, rows, hours, g):
        v = cnts[q, rows, hours, pl.ds(pl.multiple_of(g * half, half), half)]
        return v.reshape(-1, half).astype(F32)

    def anchor_step(e, before):
        left_right = jnp.concatenate([ccur[:khalf], ccur[khalf:]], axis=1)
        mixed = jnp.where(group < 2, ccur[:khalf], ccur[khalf:])
        for s in range(chunks):
            before(s)
            left = ucur[core, 8 * s:8 * s + 8]
            khs = split_kh(twice(left), left_right)
            along = None
            for g in range(2):
                values = jnp.concatenate([
                    block(core, slice(8 * s, 8 * s + 8), slice(q * khalf, (q + 1) * khalf), g)
                    for q in range(2)], axis=1)
                rh, rl = ratio_of(khs, values, g)
                part = along_of(rh, rl, g)
                along = part if along is None else along + part
            p = sum_groups(jnp.sum(along.reshape(8, khalf, LANES) * mixed[None, :, :], axis=1))
            ub = ubuf.at[e * chunks + s]
            ub[xi] = p
            start(ub, u_send.at[e * chunks + s], u_recv.at[e * chunks + s], xpeers, xi)

    def anchor_update(e):
        def update(s):
            ub = ubuf.at[e * chunks + s]
            wait_bytes(ub.at[pl.ds(0, nx - 1)], u_recv.at[e * chunks + s])
            rows = slice(8 * s, 8 * s + 8)
            for q in range(2):
                p = add_up(ub, range(q, nx, 2))
                ucur[q, rows] = ucur[q, rows] * (p / (nhour * total_cols))
        return update

    def both(s):
        rows = slice(8 * s, 8 * s + 8)
        return jnp.concatenate([ucur[0, rows], ucur[1, rows]], axis=1)

    def dest_phi(before, inner):
        dims = (((0,), (0,)), ((), ()))
        crow = 8 * nhour
        right = twice(ccur[...])
        total = None
        for s in range(chunks):
            before(s)
            if inner == 0:
                khs = split_kh(both(s), right)
                khbuf[s * crow:(s + 1) * crow] = khs
            else:
                khs = khbuf[s * crow:(s + 1) * crow]
            values = jnp.concatenate([
                block(q, slice(8 * s, 8 * s + 8), slice(None), core) for q in range(2)], axis=1)
            for r in ratio_of(khs, values, core)[:1]:
                for q in range(2):
                    lanes = slice(q * LANES, (q + 1) * LANES)
                    part = lax.dot_general(khs[:, lanes], r[:, lanes], dims, preferred_element_type=F32)
                    total = part if total is None else total + part
        return total[:rank] + total[rank:2 * rank]

    hours = pl.ds(pl.multiple_of(core * khalf, khalf), khalf)

    def hour_phi(between):
        right = twice(chour[core])
        crow = 8 * khalf
        p = None
        for order, g in enumerate((core, other)):
            if order:
                between()
            for s in range(chunks):
                left = both(s)
                if order == 0:
                    khs = split_kh(left, right)
                    khbuf[s * crow:(s + 1) * crow] = khs
                else:
                    khs = khbuf[s * crow:(s + 1) * crow]
                values = jnp.concatenate([
                    block(q, slice(8 * s, 8 * s + 8), hours, g) for q in range(2)], axis=1)
                rh, rl = ratio_of(khs, values, g)
                mixed = jnp.where(group < 2, left[:, :LANES], left[:, LANES:])
                part = jnp.sum(along_of(rh, rl, g).reshape(8, khalf, LANES) * mixed[:, None, :], axis=0)
                p = part if p is None else p + part
        return sum_groups(p)

    small[1].wait()
    wait_bytes(dbuf.at[pl.ds(0, norig - 1)], d_sem.at[1])
    tall = lax.dot_general(eye, dbuf[...].reshape(ncol, rank), (((1,), (1,)), ((), ())), precision=HIGH)
    for g in range(2):
        tcur[g] = tall[:, g * half:(g + 1) * half]
        set_right(tall[:, g * half:(g + 1) * half], g)
    for dma in large:
        dma.wait()
    ucur[core] = abuf[core]
    acopy(other).wait_recv()
    ucur[other] = abuf[other]

    @pl.loop(0, OUTER)
    def _(outer):
        before = lambda s: None
        for inner in range(INNER):
            anchor_step(outer * INNER + inner, before)
            before = anchor_update(outer * INNER + inner)

        @pl.when(outer == 0)
        def _():
            vcopy(other).wait_recv()

        anchor_w = None
        for inner in range(INNER):
            e = outer * 2 + inner
            zb, zs, zr = zbuf.at[e], z_send.at[e], z_recv.at[e]
            p = dest_phi(before, inner)
            before = lambda s: None
            col = jnp.sum(ucur[0] + ucur[1], axis=0, keepdims=True)
            zb[zi] = jnp.concatenate([p, jnp.broadcast_to(col, (8, LANES))], axis=0)
            start(zb, zs, zr, zpeers, zi)
            wait_bytes(zb.at[pl.ds(0, nz - 1)], zr)
            s = add_up(zb, range(nz))
            growth = tcur[core] * (s[:rank] / (total_rows * nhour))
            if inner == 0:
                anchor_w = s[rank:rank + 1] / total_rows
                growth = growth / to_column(anchor_w)
            else:
                tbuf[outer, core] = growth
                remote(tbuf.at[outer, core], tbuf.at[outer, core], t_sem.at[0, outer], t_sem.at[1, outer],
                       partner).start()
            tcur[core] = growth
            set_right(growth, core)
        for q in range(2):
            ucur[q] = ucur[q] / anchor_w

        def far():
            remote(tbuf.at[outer, core], tbuf.at[outer, other], t_sem.at[0, outer], t_sem.at[1, outer],
                   partner).wait_recv()
            tcur[other] = tbuf[outer, other]
            set_right(tcur[other], other)

        for q in range(2):
            chour[q] = ccur[q * khalf:(q + 1) * khalf]
        pmine = hour_phi(far)
        dest_col = to_row(jnp.sum(tcur[0] + tcur[1], axis=1, keepdims=True))
        hb, hs, hr = hbuf.at[outer], h_send.at[outer], h_recv.at[outer]
        hb[chip] = pack_hour(pmine, dest_col)
        start(hb, hs, hr, cpeers, chip)
        wait_bytes(hb.at[pl.ds(0, nchip - 1)], hr)
        s = add_up(hb, range(nchip))
        dest_w = spread_group(s[:1], copies - 1) / (total_cols * nz)
        growth = chour[core] * (unpack_hour(s) / (total_rows * total_cols)) / dest_w
        chour[core] = growth
        cbuf[outer, core] = growth
        remote(cbuf.at[outer, core], cbuf.at[outer, core], c_sem.at[0, outer], c_sem.at[1, outer], partner).start()
        pmine = hour_phi(lambda: None)
        gb, gs, gr = gbuf.at[outer], g_send.at[outer], g_recv.at[outer]
        mine = core * nchip + chip
        packed = pmine[:prow]
        for b in range(1, copies):
            packed = jnp.where(group == b, pmine[b * prow:(b + 1) * prow], packed)
        gb[mine] = packed
        for who in everyone:
            remote(gb.at[mine], gb.at[mine], gs, gr, who).start()
        remote(cbuf.at[outer, core], cbuf.at[outer, other], c_sem.at[0, outer], c_sem.at[1, outer],
               partner).wait_recv()
        chour[other] = cbuf[outer, other]
        wait_bytes(gb.at[pl.ds(0, 2 * nchip - 1)], gr)
        full = jnp.concatenate([
            chour[q] * (unpack_tight(add_up(gb, range(q * nchip, (q + 1) * nchip))) / (total_rows * total_cols))
            for q in range(2)], axis=0)
        w = jnp.sum(full, axis=0, keepdims=True) / nhour
        full = full / w
        ccur[...] = full

        @pl.when(outer == OUTER - 1)
        def _():
            anchor_out[...] = ucur[core][:, :rank]
            hour_out[...] = lax.dot_general(
                diag.astype(F32), ccur[...], (((1,), (1,)), ((), ())), precision=HIGH)
            weight_out[...] = w[:, :rank]
            place = (iota((piece, ncol), 1) == me_orig * piece + iota((piece, ncol), 0)).astype(F32)
            d = jnp.concatenate([tcur[0], tcur[1]], axis=1) / to_column(dest_w)
            dest_out[...] = lax.dot_general(place, d, (((1,), (1,)), ((), ())), precision=HIGH)

        @pl.when(outer < OUTER - 1)
        def _():
            for q in range(2):
                ucur[q] = ucur[q] * w
                tcur[q] = tcur[q] / to_column(dest_w)
                set_right(tcur[q], q)

    wait_bytes(dbuf.at[pl.ds(0, norig - 1)], d_sem.at[0])
    acopy(core).wait_send()
    vcopy(core).wait_send()
    for e in range(OUTER * INNER * chunks):
        wait_bytes(ubuf.at[e, pl.ds(0, nx - 1)], u_send.at[e])
    for e in range(OUTER * 2):
        wait_bytes(zbuf.at[e, pl.ds(0, nz - 1)], z_send.at[e])
    for e in range(OUTER):
        wait_bytes(tbuf.at[e, 0], t_sem.at[0, e])
        wait_bytes(cbuf.at[e, 0], c_sem.at[0, e])
        wait_bytes(hbuf.at[e, pl.ds(0, nchip - 1)], h_send.at[e])
        wait_bytes(gbuf.at[e, pl.ds(0, 2 * nchip - 1)], g_send.at[e])


def put_out(*refs):
    copies = [pltpu.make_async_copy(refs[q], refs[4 + q], refs[8].at[q]) for q in range(4)]
    for c in copies:
        c.start()
    for c in copies:
        c.wait()


def to_rows(row, rank):
    square = jnp.where(iota((rank, rank), 0) == iota((rank, rank), 1), jnp.broadcast_to(row, (rank, rank)), 0.0)
    return jnp.sum(square, axis=1, keepdims=True)


def on_device(counts, anchor_factor, dest_factor, hour_factor, weights):
    norig = lax.axis_size("orig")
    ndest = lax.axis_size("dest")
    nz, nx = norig // 2, 2 * ndest
    nchip = nz * ndest
    nrow, nhour, ncol = counts.shape
    rank = hour_factor.shape[1]
    khalf = nhour // 2
    chunks = nrow // 8
    hrow = -(-khalf // (8 * (LANES // rank - 1))) * 8
    prow = khalf * rank // LANES
    dma = pltpu.SemaphoreType.DMA
    vmem = pltpu.VMEM
    outs = pl.pallas_call(
        functools.partial(kernel, nz, ndest),
        out_shape=[
            jax.ShapeDtypeStruct(anchor_factor.shape, F32),
            jax.ShapeDtypeStruct(dest_factor.shape, F32),
            jax.ShapeDtypeStruct((rank, nhour), F32),
            jax.ShapeDtypeStruct((1, rank), F32),
        ],
        in_specs=[pl.BlockSpec(memory_space=pltpu.HBM)] * 5,
        out_specs=[pl.BlockSpec(memory_space=pltpu.VMEM)] * 4,
        scratch_shapes=[
            vmem((2, nrow, nhour, ncol), counts.dtype),
            vmem((2, nrow, LANES), F32),
            vmem((nhour, LANES), F32),
            vmem((2, khalf, LANES), F32),
            vmem((2, rank, LANES), F32),
            vmem((2, 2 * LANES, 2 * LANES), BF16),
            vmem((2, 4 * rank, 4 * LANES), BF16),
            vmem((nrow * nhour, 2 * LANES), BF16),
            vmem((OUTER * INNER * chunks, nx, 8, LANES), F32),
            vmem((OUTER * 2, nz, rank + 8, LANES), F32),
            vmem((OUTER, nchip, hrow, LANES), F32),
            vmem((OUTER, 2 * nchip, prow, LANES), F32),
            vmem((2, nrow, LANES), F32),
            vmem((OUTER, 2, rank, LANES), F32),
            vmem((OUTER, 2, khalf, LANES), F32),
            vmem((norig,) + dest_factor.shape, F32),
            vmem(anchor_factor.shape, F32),
            vmem((rank, nhour), F32),
            vmem((1, rank), F32),
            dma((OUTER * INNER * chunks,)), dma((OUTER * INNER * chunks,)),
            dma((OUTER * 2,)), dma((OUTER * 2,)),
            dma((OUTER,)), dma((OUTER,)),
            dma((OUTER,)), dma((OUTER,)),
            dma((2, OUTER)), dma((2, OUTER)), dma((2,)), dma((2,)), dma((2,)), dma((4 + chunks,)),
        ],
        compiler_params=pltpu.CompilerParams(
            collective_id=0, has_side_effects=True, vmem_limit_bytes=67043328),
    )(counts, anchor_factor, dest_factor, hour_factor.T, weights.reshape(1, rank))
    outs = pl.pallas_call(
        put_out,
        out_shape=[jax.ShapeDtypeStruct(o.shape, F32) for o in outs],
        in_specs=[pl.BlockSpec(memory_space=pltpu.VMEM)] * 4,
        out_specs=[pl.BlockSpec(memory_space=pltpu.HBM)] * 4,
        scratch_shapes=[dma((4,))],
    )(*outs)
    return outs[0], outs[1], outs[2].T, outs[3].reshape(rank)


def solution(mesh):
    return jax.shard_map(
        on_device,
        mesh=mesh,
        in_specs=(P("orig", None, "dest"), P("orig", None), P(("dest", "orig"), None), P(), P()),
        out_specs=(P("orig", None), P(("dest", "orig"), None), P(), P()),
        check_vma=False,
    )
```

```python
import functools

import jax
import jax.numpy as jnp
from jax import lax
from jax.experimental import pallas as pl
from jax.experimental.pallas import tpu as pltpu
from jax.sharding import PartitionSpec as P

INNER = 2
OUTER = 2
LANES = 128
F32 = jnp.float32
BF16 = jnp.bfloat16
HIGH = lax.Precision.HIGHEST
MESH = pl.DeviceIdType.MESH


def iota(shape, dim):
    return lax.broadcasted_iota(jnp.int32, shape, dim)


def kernel(nz, ndest, counts_in, anchor_in, dest_in, hour_in, weight_in,
           anchor_out, dest_out, hour_out, weight_out,
           cnts, avals, cexp, uown, ufar, ccur, bmod, balo, tmod, talo, khbuf,
           umine, ubuf, z0mine, z0buf, z1mine, z1buf, hmine, hbuf, gmine, gbuf, abuf, tbuf, cbuf, dbuf,
           anchor_ref, hour_ref, weight_ref,
           u_send, u_recv, z_send, z_recv, h_send, h_recv, g_send, g_recv, t_sem, c_sem, d_sem, a_sem, v_sem, in_sem):
    _, nrow, nhour, ncol = cnts.shape
    rank = hour_ref.shape[0]
    piece = dbuf.shape[1]
    copies = LANES // rank
    half = ncol // 2
    khalf = nhour // 2
    nx = 2 * ndest
    norig = 2 * nz
    nchip = nz * ndest
    total_rows = nrow * norig
    total_cols = ncol * ndest
    me_orig = lax.axis_index("orig")
    me_dest = lax.axis_index("dest")
    zi = me_orig // 2
    core = me_orig % 2
    other = 1 - core
    chip = zi * ndest + me_dest
    partner = {"orig": zi * 2 + other}
    chunks = nrow // 8

    up = zi * 2 // nz
    own_place = (nz - 1 - zi) * (1 - up) + zi * up
    zline = []
    for t in range(nz - 1):
        place = t + (t - own_place + nz) // nz
        zline.append((nz - 1 - place) * (1 - up) + place * up)
    zline.append(zi)
    side = 1 - 2 * (me_dest % 2)
    if ndest == 4:
        plane = [3 - me_dest, me_dest + side, (me_dest + 2) % 4, me_dest]
    else:
        plane = [(me_dest + t) % ndest for t in range(1, ndest)] + [me_dest]
    xpeers = [({"orig": zi * 2 + c, "dest": d}, k) for d in plane for k, c in enumerate((core, other))]
    xpeers = xpeers[:-2] + xpeers[-1:]
    zpeers = [({"orig": z * 2 + core}, 0) for z in zline[:-1]]
    opeers = [{"orig": z * 2 + c} for z in zline for c in (core, other)]
    opeers = opeers[:-2] + opeers[-1:]
    everyone = [({"orig": z * 2 + c, "dest": d}, k) for z in zline for d in plane for k, c in enumerate((core, other))]
    everyone = everyone[:-2] + everyone[-1:]
    cpeers = [who for who in everyone if who[1] == 0]

    small = [pltpu.make_async_copy(a, b, in_sem.at[q]) for q, (a, b) in enumerate(
        ((anchor_in, anchor_ref), (dest_in, dbuf.at[me_orig]), (hour_in, hour_ref), (weight_in, weight_ref)))]
    large = [pltpu.make_async_copy(counts_in.at[pl.ds(8 * s, 8)], cnts.at[0, pl.ds(8 * s, 8)], in_sem.at[4 + s])
             for s in range(chunks)]
    for dma in small + large:
        dma.start()
    barrier = pltpu.get_barrier_semaphore()
    near = opeers[:-1] + [who for who, _ in xpeers]
    for who in near:
        pl.semaphore_signal(barrier, inc=1, device_id=who, device_id_type=MESH)

    def remote(src, dst, send, recv, who):
        return pltpu.make_async_remote_copy(
            src_ref=src, dst_ref=dst, send_sem=send, recv_sem=recv, device_id=who, device_id_type=MESH)

    def start(mine, ref, send, recv, peers, slot, n):
        for who, far in peers:
            remote(mine, ref.at[slot + n * far], send, recv, who).start()

    def wait_bytes(ref, sem):
        pltpu.make_async_copy(ref, ref, sem).wait()

    def add_up(ref, slots, total):
        parts = [ref[s] for s in slots] + ([] if total is None else [total])
        while len(parts) > 1:
            parts = [a + b for a, b in zip(parts[::2], parts[1::2])] + parts[len(parts) // 2 * 2:]
        return parts[0]

    lane = iota((1, LANES), 1)
    group = lane // rank
    spread = (iota((rank, LANES), 1) % rank == iota((rank, LANES), 0)).astype(F32)
    diag = iota((rank, LANES), 1) == iota((rank, LANES), 0)
    diag_all = iota((rank, LANES), 1) % rank == iota((rank, LANES), 0)
    eye = (iota((rank, rank), 0) == iota((rank, rank), 1)).astype(F32)

    def to_column(row):
        return jnp.sum(jnp.where(diag, jnp.broadcast_to(row, (rank, LANES)), 0.0), axis=1, keepdims=True)

    def to_row(column):
        return jnp.sum(jnp.where(diag_all, jnp.broadcast_to(column, (rank, LANES)), 0.0), axis=0, keepdims=True)

    def sum_groups(x):
        step = rank
        while step < LANES:
            x = x + pltpu.roll(x, step, 1)
            step *= 2
        return x

    def spread_group(x, b):
        return sum_groups(jnp.where(group == b, x, 0.0))

    def pair_up(x):
        return x + pltpu.roll(x, rank, 1)

    def twice(x):
        return jnp.concatenate([x, x], axis=1)

    hrow = hbuf.shape[2]
    prow = gbuf.shape[2]
    hblocks = khalf // hrow

    def pack_hour(p, extra):
        out = jnp.broadcast_to(extra, (hrow, LANES))
        for b in range(hblocks):
            out = jnp.where(group == b, p[b * hrow:(b + 1) * hrow], out)
        return out

    def unpack_hour(s):
        return jnp.concatenate([spread_group(s, b) for b in range(hblocks)], axis=0)

    def pack_tight(p):
        out = p[:prow]
        for b in range(1, copies):
            out = jnp.where(group == b, p[b * prow:(b + 1) * prow], out)
        return out

    def unpack_tight(s):
        return jnp.concatenate([spread_group(s, b) for b in range(copies)], axis=0)

    def set_hours(c):
        ccur[...] = c
        cexp[...] = jnp.broadcast_to(c[:, None, :], (nhour, 8, LANES)).reshape(8 * nhour, LANES)

    for dma in (small[0], small[2], small[3]):
        dma.wait()
    weight_row = jnp.sum(jnp.where(
        diag_all, jnp.broadcast_to(to_rows(weight_ref[...], rank), (rank, LANES)), 0.0), axis=0, keepdims=True)
    own_anchor = lax.dot(anchor_ref[...], spread, precision=HIGH) * weight_row
    abuf[0] = own_anchor
    uown[...] = own_anchor
    set_hours(lax.dot_general(hour_ref[...], spread, (((0,), (0,)), ((), ())), precision=HIGH))
    bmod[...] = jnp.zeros_like(bmod)
    balo[...] = jnp.zeros_like(balo)
    for ref, slot in ((ubuf, me_dest), (z0buf, zi), (z1buf, zi), (hbuf, chip), (gbuf, chip)):
        for e in range(ref.shape[0]):
            ref[e, slot] = jnp.zeros(ref.shape[2:], F32)

    pl.semaphore_wait(barrier, len(near))

    for who in opeers:
        remote(dest_in, dbuf.at[me_orig], d_sem.at[0], d_sem.at[1], who).start()
    acopy = remote(abuf.at[0], abuf.at[1], a_sem.at[0], a_sem.at[1], partner)
    vcopy = remote(counts_in, cnts.at[1], v_sem.at[0], v_sem.at[1], partner)
    acopy.start()
    vcopy.start()

    def split(t):
        hi = t.astype(BF16).astype(F32)
        return hi, t - hi

    def set_block(t, g):
        hi, lo = split(t)
        model = jnp.concatenate([hi] * (copies // 2) + [lo] * (copies // 2), axis=0).astype(BF16)
        for q in range(2):
            lanes = slice(q * LANES, (q + 1) * LANES)
            bmod[g, lanes, lanes] = model

    def set_along(t, g):
        along = jnp.concatenate(split(t), axis=0).astype(BF16)
        for q in range(2):
            balo[g, q * 2 * rank:(q + 1) * 2 * rank, q * LANES:(q + 1) * LANES] = along

    def set_whole(t, g):
        hi, lo = split(t)
        lanes = slice(g * half, (g + 1) * half)
        tmod[:, lanes] = jnp.concatenate([hi] * (copies // 2) + [lo] * (copies // 2), axis=0).astype(BF16)
        talo[:, lanes] = jnp.concatenate([hi, lo] * (copies // 2), axis=0).astype(BF16)

    high_lane = (iota((1, LANES), 1) // rank) % 2 == 0
    high_lanes = (iota((1, 2 * LANES), 1) // rank) % 2 == 0

    def split_low(kh, high):
        hi = kh.astype(BF16).astype(F32)
        return jnp.where(high, hi, kh - hi).astype(BF16)

    def block_kh(left, right):
        kh = (left[:, None, :] * right[None, :, :]).reshape(left.shape[0] * right.shape[0], 2 * LANES)
        return split_low(kh, high_lanes)

    def ratio_of(khs, values, right):
        model = jnp.dot(khs, right, preferred_element_type=F32)
        return (values / model).astype(BF16)

    def along_of(r, right):
        return lax.dot_general(r, right, (((1,), (1,)), ((), ())), preferred_element_type=F32)

    sides = [pl.ds(pl.multiple_of(c * half, half), half) for c in (core, other)]
    hours = pl.ds(pl.multiple_of(core * khalf, khalf), khalf)

    def block(s, hrs, g):
        return jnp.concatenate([
            cnts[q, 8 * s:8 * s + 8, hrs, sides[g]].reshape(-1, half).astype(F32) for q in range(2)], axis=1)

    def anchor_step(e, before):
        mine = []
        for s in range(chunks):
            before(s)
            left = uown[8 * s:8 * s + 8]
            kh = (left[None] * cexp[...].reshape(nhour, 8, LANES)).reshape(8 * nhour, LANES)
            r = ratio_of(split_low(kh, high_lane), avals[s], tmod[...])
            p = pair_up(jnp.sum((along_of(r, talo[...]) * cexp[...]).reshape(nhour, 8, LANES), axis=0))
            at = e * chunks + s
            umine[at] = p
            start(umine.at[at], ubuf.at[at], u_send.at[at], u_recv.at[at], xpeers, me_dest, ndest)
            mine.append(p)
        return mine

    def anchor_update(e, mine):
        def update(s):
            at = e * chunks + s
            if e == 0 and s == 0:
                acopy.wait_recv()
                ufar[...] = abuf[1]
            wait_bytes(ubuf.at[at, pl.ds(0, nx - 1)], u_recv.at[at])
            rows = slice(8 * s, 8 * s + 8)
            p = add_up(ubuf.at[at], range(ndest), mine[s])
            uown[rows] = uown[rows] * (p * (1.0 / (nhour * total_cols)))
            p = add_up(ubuf.at[at], range(ndest, nx), None)
            ufar[rows] = ufar[rows] * (p * (1.0 / (nhour * total_cols)))
        return update

    def both(s):
        rows = slice(8 * s, 8 * s + 8)
        return jnp.concatenate([uown[rows], ufar[rows]], axis=1)

    def dest_phi(before, inner):
        crow = 8 * nhour
        right = twice(ccur[...])
        total = None
        for s in range(chunks):
            before(s)
            if inner == 0:
                khs = block_kh(both(s), right)
                khbuf[s * crow:(s + 1) * crow] = khs
            else:
                khs = khbuf[s * crow:(s + 1) * crow]
            r = ratio_of(khs, block(s, slice(None), 0), bmod[0])
            for q in range(2):
                lanes = slice(q * LANES, (q + 1) * LANES)
                part = lax.dot_general(
                    khs[:, lanes], r[:, lanes], (((0,), (0,)), ((), ())), preferred_element_type=F32)
                total = part if total is None else total + part
        return total[:rank] + total[rank:2 * rank]

    def hour_phi(c, between):
        right = twice(c)
        crow = 8 * khalf
        p = None
        for g in range(2):
            if g:
                between()
            for s in range(chunks):
                left = both(s)
                if g == 0:
                    khs = block_kh(left, right)
                    khbuf[s * crow:(s + 1) * crow] = khs
                else:
                    khs = khbuf[s * crow:(s + 1) * crow]
                r = ratio_of(khs, block(s, hours, g), bmod[g])
                mixed = jnp.where(group < 2, left[:, :LANES], left[:, LANES:])
                part = jnp.sum(along_of(r, balo[g]).reshape(8, khalf, LANES) * mixed[:, None, :], axis=0)
                p = part if p is None else p + part
        return sum_groups(p)

    for s in range(chunks):
        large[s].wait()
        for g in range(2):
            v = cnts[0, 8 * s:8 * s + 8, :, sides[g]].astype(F32)
            avals[s, :, g * half:(g + 1) * half] = jnp.swapaxes(v, 0, 1).reshape(8 * nhour, half)

    small[1].wait()
    wait_bytes(dbuf.at[pl.ds(0, norig - 1)], d_sem.at[1])
    tcur = []
    for g, c in enumerate((core, other)):
        d = dbuf[pl.ds(c * nz, nz)].reshape(half, rank)
        tcur.append(lax.dot_general(eye, d, (((1,), (1,)), ((), ())), precision=HIGH))
        set_whole(tcur[g], g)

    dest_w = None
    chour = None
    for outer in range(OUTER):
        before = lambda s: None
        for inner in range(INNER):
            mine = anchor_step(outer * INNER + inner, before)
            before = anchor_update(outer * INNER + inner, mine)
            if inner == 0:
                set_block(tcur[0], 0)
                if chour is None:
                    chour = [jnp.where(core == k, ccur[:khalf], ccur[khalf:]) for k in range(2)]
        if outer == 0:
            vcopy.wait_recv()

        anchor_w = None
        for inner in range(INNER):
            e = outer * 2 + inner
            own, zb = ((z0mine, z0buf), (z1mine, z1buf))[inner]
            p = dest_phi(before, inner)
            before = lambda s: None
            send = p
            if inner == 0:
                col = jnp.sum(uown[...] + ufar[...], axis=0, keepdims=True)
                send = jnp.concatenate([p, jnp.broadcast_to(col, (8, LANES))], axis=0)
            own[outer] = send
            start(own.at[outer], zb.at[outer], z_send.at[e], z_recv.at[e], zpeers, zi, 0)
            wait_bytes(zb.at[outer, pl.ds(0, nz - 1)], z_recv.at[e])
            s = add_up(zb.at[outer], range(nz), send)
            growth = tcur[0] * (s[:rank] * (1.0 / (total_rows * nhour)))
            if inner == 0:
                anchor_w = s[rank:rank + 1] * (1.0 / total_rows)
                growth = growth * to_column((1.0 if dest_w is None else dest_w) / anchor_w)
            else:
                tbuf[outer, 0] = growth
                remote(tbuf.at[outer, 0], tbuf.at[outer, 1], t_sem.at[0, outer], t_sem.at[1, outer], partner).start()
                set_along(growth, 0)
            tcur[0] = growth
            set_block(growth, 0)
            if inner == 0:
                inv = 1.0 / anchor_w
        uown[...] = uown[...] * inv
        ufar[...] = ufar[...] * inv

        def far():
            remote(tbuf.at[outer, 0], tbuf.at[outer, 1], t_sem.at[0, outer], t_sem.at[1, outer], partner).wait_recv()
            tcur[1] = tbuf[outer, 1]
            set_block(tcur[1], 1)
            set_along(tcur[1], 1)

        pmine = hour_phi(chour[0], far)
        dest_col = to_row(jnp.sum(tcur[0] + tcur[1], axis=1, keepdims=True))
        send = pack_hour(pmine, dest_col)
        hmine[outer] = send
        start(hmine.at[outer], hbuf.at[outer], h_send.at[outer], h_recv.at[outer], cpeers, chip, 0)
        if outer < OUTER - 1:
            for g in range(2):
                set_whole(tcur[g], g)
        wait_bytes(hbuf.at[outer, pl.ds(0, nchip - 1)], h_recv.at[outer])
        s = add_up(hbuf.at[outer], range(nchip), send)
        dest_w = spread_group(s[:1], copies - 1) * (1.0 / (total_cols * nz))
        growth = chour[0] * (unpack_hour(s) * (1.0 / (total_rows * total_cols))) / dest_w
        cbuf[outer, 0] = growth
        remote(cbuf.at[outer, 0], cbuf.at[outer, 1], c_sem.at[0, outer], c_sem.at[1, outer], partner).start()
        pmine = hour_phi(growth, lambda: None)
        send = pack_tight(pmine)
        gmine[outer] = send
        start(gmine.at[outer], gbuf.at[outer], g_send.at[outer], g_recv.at[outer], everyone, chip, nchip)
        remote(cbuf.at[outer, 0], cbuf.at[outer, 1], c_sem.at[0, outer], c_sem.at[1, outer], partner).wait_recv()
        wait_bytes(gbuf.at[outer, pl.ds(0, 2 * nchip - 1)], g_recv.at[outer])
        chour = [
            c * (unpack_tight(add_up(gbuf.at[outer], range(q * nchip, (q + 1) * nchip), (send, None)[q]))
                 * (1.0 / (total_rows * total_cols)))
            for q, c in enumerate((growth, cbuf[outer, 1]))]
        w = jnp.sum(chour[0] + chour[1], axis=0, keepdims=True) * (1.0 / nhour)
        chour = [c / w for c in chour]
        hour = jnp.concatenate([jnp.where(core == k, chour[0], chour[1]) for k in range(2)], axis=0)
        if outer < OUTER - 1:
            set_hours(hour / dest_w)
            uown[...] = uown[...] * w
            ufar[...] = ufar[...] * w

    anchor_out[...] = uown[:, :rank]
    hour_out[...] = lax.dot_general(diag.astype(F32), hour, (((1,), (1,)), ((), ())), precision=HIGH)
    weight_out[...] = w[:, :rank]
    at = iota((piece, ncol), 1)
    at = (at // half + core) % 2 * half + at % half
    place = (at == me_orig * piece + iota((piece, ncol), 0)).astype(F32)
    d = jnp.concatenate(tcur, axis=1) / to_column(dest_w)
    dest_out[...] = lax.dot_general(place, d, (((1,), (1,)), ((), ())), precision=HIGH)

    wait_bytes(dbuf.at[pl.ds(0, norig - 1)], d_sem.at[0])
    acopy.wait_send()
    vcopy.wait_send()
    for e in range(OUTER * INNER * chunks):
        wait_bytes(ubuf.at[e, pl.ds(0, nx - 1)], u_send.at[e])
    for e in range(OUTER):
        wait_bytes(z0buf.at[e, pl.ds(0, nz - 1)], z_send.at[2 * e])
        wait_bytes(z1buf.at[e, pl.ds(0, nz - 1)], z_send.at[2 * e + 1])
        wait_bytes(tbuf.at[e, 0], t_sem.at[0, e])
        wait_bytes(cbuf.at[e, 0], c_sem.at[0, e])
        wait_bytes(hbuf.at[e, pl.ds(0, nchip - 1)], h_send.at[e])
        wait_bytes(gbuf.at[e, pl.ds(0, 2 * nchip - 1)], g_send.at[e])


def put_out(*refs):
    copies = [pltpu.make_async_copy(refs[q], refs[4 + q], refs[8].at[q]) for q in range(4)]
    for c in copies:
        c.start()
    for c in copies:
        c.wait()


def to_rows(row, rank):
    square = jnp.where(iota((rank, rank), 0) == iota((rank, rank), 1), jnp.broadcast_to(row, (rank, rank)), 0.0)
    return jnp.sum(square, axis=1, keepdims=True)


def on_device(counts, anchor_factor, dest_factor, hour_factor, weights):
    norig = lax.axis_size("orig")
    ndest = lax.axis_size("dest")
    nz, nx = norig // 2, 2 * ndest
    nchip = nz * ndest
    nrow, nhour, ncol = counts.shape
    rank = hour_factor.shape[1]
    khalf = nhour // 2
    chunks = nrow // 8
    hrow = -(-khalf // (8 * (LANES // rank - 1))) * 8
    prow = khalf * rank // LANES
    dma = pltpu.SemaphoreType.DMA
    vmem = pltpu.VMEM
    outs = pl.pallas_call(
        functools.partial(kernel, nz, ndest),
        out_shape=[
            jax.ShapeDtypeStruct(anchor_factor.shape, F32),
            jax.ShapeDtypeStruct(dest_factor.shape, F32),
            jax.ShapeDtypeStruct((rank, nhour), F32),
            jax.ShapeDtypeStruct((1, rank), F32),
        ],
        in_specs=[pl.BlockSpec(memory_space=pltpu.HBM)] * 5,
        out_specs=[pl.BlockSpec(memory_space=pltpu.VMEM)] * 4,
        scratch_shapes=[
            vmem((2, nrow, nhour, ncol), counts.dtype),
            vmem((chunks, 8 * nhour, ncol), F32),
            vmem((8 * nhour, LANES), F32),
            vmem((nrow, LANES), F32),
            vmem((nrow, LANES), F32),
            vmem((nhour, LANES), F32),
            vmem((2, 2 * LANES, 2 * LANES), BF16),
            vmem((2, 4 * rank, 2 * LANES), BF16),
            vmem((LANES, ncol), BF16),
            vmem((LANES, ncol), BF16),
            vmem((nrow * nhour, 2 * LANES), BF16),
            vmem((OUTER * INNER * chunks, 8, LANES), F32),
            vmem((OUTER * INNER * chunks, nx, 8, LANES), F32),
            vmem((OUTER, rank + 8, LANES), F32),
            vmem((OUTER, nz, rank + 8, LANES), F32),
            vmem((OUTER, rank, LANES), F32),
            vmem((OUTER, nz, rank, LANES), F32),
            vmem((OUTER, hrow, LANES), F32),
            vmem((OUTER, nchip, hrow, LANES), F32),
            vmem((OUTER, prow, LANES), F32),
            vmem((OUTER, 2 * nchip, prow, LANES), F32),
            vmem((2, nrow, LANES), F32),
            vmem((OUTER, 2, rank, LANES), F32),
            vmem((OUTER, 2, khalf, LANES), F32),
            vmem((norig,) + dest_factor.shape, F32),
            vmem(anchor_factor.shape, F32),
            vmem((rank, nhour), F32),
            vmem((1, rank), F32),
            dma((OUTER * INNER * chunks,)), dma((OUTER * INNER * chunks,)),
            dma((OUTER * 2,)), dma((OUTER * 2,)),
            dma((OUTER,)), dma((OUTER,)),
            dma((OUTER,)), dma((OUTER,)),
            dma((2, OUTER)), dma((2, OUTER)), dma((2,)), dma((2,)), dma((2,)), dma((4 + chunks,)),
        ],
        compiler_params=pltpu.CompilerParams(
            collective_id=0, has_side_effects=True, vmem_limit_bytes=67043328),
    )(counts, anchor_factor, dest_factor, hour_factor.T, weights.reshape(1, rank))
    outs = pl.pallas_call(
        put_out,
        out_shape=[jax.ShapeDtypeStruct(o.shape, F32) for o in outs],
        in_specs=[pl.BlockSpec(memory_space=pltpu.VMEM)] * 4,
        out_specs=[pl.BlockSpec(memory_space=pltpu.HBM)] * 4,
        scratch_shapes=[dma((4,))],
    )(*outs)
    return outs[0], outs[1], outs[2].T, outs[3].reshape(rank)


def solution(mesh):
    return jax.shard_map(
        on_device,
        mesh=mesh,
        in_specs=(P("orig", None, "dest"), P("orig", None), P(("dest", "orig"), None), P(), P()),
        out_specs=(P("orig", None), P(("dest", "orig"), None), P(), P()),
        check_vma=False,
    )
```

```python
import functools

import jax
import jax.numpy as jnp
from jax import lax
from jax.experimental import pallas as pl
from jax.experimental.pallas import tpu as pltpu
from jax.sharding import PartitionSpec as P

INNER = 2
OUTER = 2
LANES = 128
F32 = jnp.float32
BF16 = jnp.bfloat16
HIGH = lax.Precision.HIGHEST
MESH = pl.DeviceIdType.MESH


def iota(shape, dim):
    return lax.broadcasted_iota(jnp.int32, shape, dim)


def kernel(nz, ndest, counts_in, anchor_in, dest_in, hour_in, weight_in,
           anchor_out, dest_out, hour_out, weight_out,
           cnts, avals, cexp, uown, ufar, ccur, bmod, balo, tmod, talo, khbuf,
           umine, ubuf, wmine, wbuf, zmine, zbuf, hmine, hbuf, gmine, gbuf, abuf, tbuf, cbuf, dbuf,
           anchor_ref, hour_ref, weight_ref,
           u_send, u_recv, w_send, w_recv, z_send, z_recv, h_send, h_recv, g_send, g_recv, t_sem, c_sem, d_sem, a_sem, v_sem, in_sem):
    _, nrow, nhour, ncol = cnts.shape
    rank = hour_ref.shape[0]
    piece = dbuf.shape[1]
    copies = LANES // rank
    half = ncol // 2
    khalf = nhour // 2
    nx = 2 * ndest
    norig = 2 * nz
    nchip = nz * ndest
    total_rows = nrow * norig
    total_cols = ncol * ndest
    me_orig = lax.axis_index("orig")
    me_dest = lax.axis_index("dest")
    zi = me_orig // 2
    core = me_orig % 2
    other = 1 - core
    chip = zi * ndest + me_dest
    partner = {"orig": zi * 2 + other}
    chunks = nrow // 8

    up = zi * 2 // nz
    own_place = (nz - 1 - zi) * (1 - up) + zi * up
    zline = []
    for t in range(nz - 1):
        place = t + (t - own_place + nz) // nz
        zline.append((nz - 1 - place) * (1 - up) + place * up)
    zline.append(zi)
    side = 1 - 2 * (me_dest % 2)
    if ndest == 4:
        plane = [3 - me_dest, me_dest + side, (me_dest + 2) % 4, me_dest]
    else:
        plane = [(me_dest + t) % ndest for t in range(1, ndest)] + [me_dest]
    xpeers = [({"orig": zi * 2 + c, "dest": d}, k) for d in plane for k, c in enumerate((core, other))]
    xpeers = xpeers[:-2] + xpeers[-1:]
    zpeers = [({"orig": z * 2 + core}, 0) for z in zline[:-1]]
    opeers = [{"orig": z * 2 + c} for z in zline for c in (core, other)]
    opeers = opeers[:-2] + opeers[-1:]
    everyone = [({"orig": z * 2 + c, "dest": d}, k) for z in zline for d in plane for k, c in enumerate((core, other))]
    everyone = everyone[:-2] + everyone[-1:]
    cpeers = [who for who in everyone if who[1] == 0]

    small = [pltpu.make_async_copy(a, b, in_sem.at[q]) for q, (a, b) in enumerate(
        ((anchor_in, anchor_ref), (dest_in, dbuf.at[me_orig]), (hour_in, hour_ref), (weight_in, weight_ref)))]
    large = [pltpu.make_async_copy(counts_in.at[pl.ds(8 * s, 8)], cnts.at[0, pl.ds(8 * s, 8)], in_sem.at[4 + s])
             for s in range(chunks)]
    for dma in small + large:
        dma.start()
    barrier = pltpu.get_barrier_semaphore()
    near = opeers[:-1] + [who for who, _ in xpeers]
    for who in near:
        pl.semaphore_signal(barrier, inc=1, device_id=who, device_id_type=MESH)

    def remote(src, dst, send, recv, who):
        return pltpu.make_async_remote_copy(
            src_ref=src, dst_ref=dst, send_sem=send, recv_sem=recv, device_id=who, device_id_type=MESH)

    def start(mine, ref, send, recv, peers, slot, n):
        for who, far in peers:
            remote(mine, ref.at[slot + n * far], send, recv, who).start()

    def wait_bytes(ref, sem):
        pltpu.make_async_copy(ref, ref, sem).wait()

    def add_up(ref, slots, total):
        parts = [ref[s] for s in slots] + ([] if total is None else [total])
        while len(parts) > 1:
            parts = [a + b for a, b in zip(parts[::2], parts[1::2])] + parts[len(parts) // 2 * 2:]
        return parts[0]

    lane = iota((1, LANES), 1)
    group = lane // rank
    spread = (iota((rank, LANES), 1) % rank == iota((rank, LANES), 0)).astype(F32)
    diag = iota((rank, LANES), 1) == iota((rank, LANES), 0)
    diag_all = iota((rank, LANES), 1) % rank == iota((rank, LANES), 0)

    def to_column(row):
        return jnp.sum(jnp.where(diag, jnp.broadcast_to(row, (rank, LANES)), 0.0), axis=1, keepdims=True)

    def to_row(column):
        return jnp.sum(jnp.where(diag_all, jnp.broadcast_to(column, (rank, LANES)), 0.0), axis=0, keepdims=True)

    def sum_groups(x):
        step = rank
        while step < LANES:
            x = x + pltpu.roll(x, step, 1)
            step *= 2
        return x

    def spread_group(x, b):
        return sum_groups(jnp.where(group == b, x, 0.0))

    def pair_up(x):
        return x + pltpu.roll(x, rank, 1)

    def twice(x):
        return jnp.concatenate([x, x], axis=1)

    hrow = hbuf.shape[2]
    prow = gbuf.shape[2]
    hblocks = khalf // hrow

    def pack_hour(p, extra):
        out = jnp.broadcast_to(extra, (hrow, LANES))
        for b in range(hblocks):
            out = jnp.where(group == b, p[b * hrow:(b + 1) * hrow], out)
        return out

    def unpack_hour(s):
        return jnp.concatenate([spread_group(s, b) for b in range(hblocks)], axis=0)

    def pack_tight(p):
        out = p[:prow]
        for b in range(1, copies):
            out = jnp.where(group == b, p[b * prow:(b + 1) * prow], out)
        return out

    def unpack_tight(s):
        return jnp.concatenate([spread_group(s, b) for b in range(copies)], axis=0)

    def set_hours(c):
        ccur[...] = c
        cexp[...] = jnp.broadcast_to(c[:, None, :], (nhour, 8, LANES)).reshape(8 * nhour, LANES)

    for dma in (small[0], small[2], small[3]):
        dma.wait()
    weight_row = jnp.sum(jnp.where(
        diag_all, jnp.broadcast_to(to_rows(weight_ref[...], rank), (rank, LANES)), 0.0), axis=0, keepdims=True)
    own_anchor = lax.dot(anchor_ref[...], spread, precision=HIGH) * weight_row
    abuf[0] = own_anchor
    uown[...] = own_anchor
    set_hours(lax.dot_general(hour_ref[...], spread, (((0,), (0,)), ((), ())), precision=HIGH))
    bmod[...] = jnp.zeros_like(bmod)
    balo[...] = jnp.zeros_like(balo)
    for ref, slot in ((ubuf, me_dest), (wbuf, zi), (zbuf, zi), (hbuf, chip), (gbuf, chip)):
        for e in range(ref.shape[0]):
            ref[e, slot] = jnp.zeros(ref.shape[2:], F32)

    small[1].wait()
    pl.semaphore_wait(barrier, len(near))

    for who in opeers:
        remote(dbuf.at[me_orig], dbuf.at[me_orig], d_sem.at[0], d_sem.at[1], who).start()
    acopy = remote(abuf.at[0], abuf.at[1], a_sem.at[0], a_sem.at[1], partner)
    vcopy = remote(counts_in, cnts.at[1], v_sem.at[0], v_sem.at[1], partner)
    acopy.start()

    def split(t):
        hi = t.astype(BF16).astype(F32)
        return hi, t - hi

    def set_block(t, g):
        hi, lo = split(t)
        model = jnp.concatenate([hi] * (copies // 2) + [lo] * (copies // 2), axis=0).astype(BF16)
        for q in range(2):
            lanes = slice(q * LANES, (q + 1) * LANES)
            bmod[g, lanes, lanes] = model

    def set_along(t, g):
        along = jnp.concatenate(split(t), axis=0).astype(BF16)
        for q in range(2):
            balo[g, q * 2 * rank:(q + 1) * 2 * rank, q * LANES:(q + 1) * LANES] = along

    def set_whole(t, g):
        hi, lo = split(t)
        lanes = slice(g * half, (g + 1) * half)
        tmod[:, lanes] = jnp.concatenate([hi] * (copies // 2) + [lo] * (copies // 2), axis=0).astype(BF16)
        talo[:, lanes] = jnp.concatenate([hi, lo] * (copies // 2), axis=0).astype(BF16)

    high_lane = (iota((1, LANES), 1) // rank) % 2 == 0
    high_lanes = (iota((1, 2 * LANES), 1) // rank) % 2 == 0

    def split_low(kh, high):
        hi = kh.astype(BF16).astype(F32)
        return jnp.where(high, hi, kh - hi).astype(BF16)

    def block_kh(left, right):
        kh = (left[:, None, :] * right[None, :, :]).reshape(left.shape[0] * right.shape[0], 2 * LANES)
        return split_low(kh, high_lanes)

    def ratio_of(khs, values, right):
        model = jnp.dot(khs, right, preferred_element_type=F32)
        return (values / model).astype(BF16)

    def along_of(r, right):
        return lax.dot_general(r, right, (((1,), (1,)), ((), ())), preferred_element_type=F32)

    sides = [pl.ds(pl.multiple_of(c * half, half), half) for c in (core, other)]
    hours = pl.ds(pl.multiple_of(core * khalf, khalf), khalf)

    def block(s, hrs, g):
        return jnp.concatenate([
            cnts[q, 8 * s:8 * s + 8, hrs, sides[g]].reshape(-1, half).astype(F32) for q in range(2)], axis=1)

    def anchor_step(e, before):
        mine = []
        for s in range(chunks):
            before(s)
            left = uown[8 * s:8 * s + 8]
            kh = (left[None] * cexp[...].reshape(nhour, 8, LANES)).reshape(8 * nhour, LANES)
            r = ratio_of(split_low(kh, high_lane), avals[s], tmod[...])
            p = pair_up(jnp.sum((along_of(r, talo[...]) * cexp[...]).reshape(nhour, 8, LANES), axis=0))
            at = e * chunks + s
            umine[at] = p
            start(umine.at[at], ubuf.at[at], u_send.at[at], u_recv.at[at], xpeers, me_dest, ndest)
            mine.append(p)
        return mine

    def anchor_update(e, mine):
        def update(s):
            at = e * chunks + s
            if e == 0 and s == 0:
                acopy.wait_recv()
                ufar[...] = abuf[1]
            wait_bytes(ubuf.at[at, pl.ds(0, nx - 1)], u_recv.at[at])
            rows = slice(8 * s, 8 * s + 8)
            p = add_up(ubuf.at[at], range(ndest), mine[s])
            uown[rows] = uown[rows] * (p * (1.0 / (nhour * total_cols)))
            p = add_up(ubuf.at[at], range(ndest, nx), None)
            ufar[rows] = ufar[rows] * (p * (1.0 / (nhour * total_cols)))
        return update

    def both(s):
        rows = slice(8 * s, 8 * s + 8)
        return jnp.concatenate([uown[rows], ufar[rows]], axis=1)

    def dest_phi(before, inner):
        crow = 8 * nhour
        right = twice(ccur[...])
        total = None
        for s in range(chunks):
            if inner == 0:
                before(s)
                khs = block_kh(both(s), right)
                khbuf[s * crow:(s + 1) * crow] = khs
            else:
                khs = khbuf[s * crow:(s + 1) * crow]
            r = ratio_of(khs, block(s, slice(None), 0), bmod[0])
            for q in range(2):
                lanes = slice(q * LANES, (q + 1) * LANES)
                part = lax.dot_general(
                    khs[:, lanes], r[:, lanes], (((0,), (0,)), ((), ())), preferred_element_type=F32)
                total = part if total is None else total + part
        return total[:rank] + total[rank:2 * rank]

    def hour_phi(c, between):
        right = twice(c)
        crow = 8 * khalf
        p = None
        for g in range(2):
            if g:
                between()
            for s in range(chunks):
                left = both(s)
                if g == 0:
                    khs = block_kh(left, right)
                    khbuf[s * crow:(s + 1) * crow] = khs
                else:
                    khs = khbuf[s * crow:(s + 1) * crow]
                r = ratio_of(khs, block(s, hours, g), bmod[g])
                mixed = jnp.where(group < 2, left[:, :LANES], left[:, LANES:])
                part = jnp.sum(along_of(r, balo[g]).reshape(8, khalf, LANES) * mixed[:, None, :], axis=0)
                p = part if p is None else p + part
        return sum_groups(p)

    for s in range(chunks):
        large[s].wait()
        for g in range(2):
            v = cnts[0, 8 * s:8 * s + 8, :, sides[g]].astype(F32)
            avals[s, :, g * half:(g + 1) * half] = jnp.swapaxes(v, 0, 1).reshape(8 * nhour, half)

    wait_bytes(dbuf.at[pl.ds(0, norig - 1)], d_sem.at[1])
    tcur = []
    for g, c in enumerate((core, other)):
        d = dbuf[pl.ds(c * nz, nz)].reshape(half, rank)
        tcur.append(jnp.transpose(d))
        set_whole(tcur[g], g)

    dest_w = None
    chour = None
    for outer in range(OUTER):
        before = lambda s: None
        for inner in range(INNER):
            mine = anchor_step(outer * INNER + inner, before)
            before = anchor_update(outer * INNER + inner, mine)
            if outer + inner == 0:
                vcopy.start()
            if inner == 0:
                set_block(tcur[0], 0)
                if chour is None:
                    chour = [jnp.where(core == k, ccur[:khalf], ccur[khalf:]) for k in range(2)]
        if outer == 0:
            vcopy.wait_recv()

        def settle(s):
            before(s)
            if s == chunks - 1:
                col = jnp.broadcast_to(jnp.sum(uown[...] + ufar[...], axis=0, keepdims=True), (8, LANES))
                wmine[outer] = col
                start(wmine.at[outer], wbuf.at[outer], w_send.at[outer], w_recv.at[outer], zpeers, zi, 0)

        for inner in range(INNER):
            e = outer * 2 + inner
            p = dest_phi(settle, inner)
            zmine[e] = p
            start(zmine.at[e], zbuf.at[e], z_send.at[e], z_recv.at[e], zpeers, zi, 0)
            if inner == 0:
                wait_bytes(wbuf.at[outer, pl.ds(0, nz - 1)], w_recv.at[outer])
                inv = (1.0 * total_rows) / add_up(wbuf.at[outer], range(nz), wmine[outer])[:1]
                old = tcur[0] * (to_column(inv if dest_w is None else inv * dest_w) * (1.0 / (total_rows * nhour)))
            else:
                old = tcur[0] * (1.0 / (total_rows * nhour))
                uown[...] = uown[...] * inv
                ufar[...] = ufar[...] * inv
            wait_bytes(zbuf.at[e, pl.ds(0, nz - 1)], z_recv.at[e])
            growth = old * add_up(zbuf.at[e], range(nz), p)
            if inner:
                tbuf[outer, 0] = growth
                remote(tbuf.at[outer, 0], tbuf.at[outer, 1], t_sem.at[0, outer], t_sem.at[1, outer], partner).start()
                set_along(growth, 0)
            tcur[0] = growth
            set_block(growth, 0)

        def far():
            remote(tbuf.at[outer, 0], tbuf.at[outer, 1], t_sem.at[0, outer], t_sem.at[1, outer], partner).wait_recv()
            tcur[1] = tbuf[outer, 1]
            set_block(tcur[1], 1)
            set_along(tcur[1], 1)

        pmine = hour_phi(chour[0], far)
        dest_col = to_row(jnp.sum(tcur[0] + tcur[1], axis=1, keepdims=True))
        send = pack_hour(pmine, dest_col)
        hmine[outer] = send
        start(hmine.at[outer], hbuf.at[outer], h_send.at[outer], h_recv.at[outer], cpeers, chip, 0)
        if outer < OUTER - 1:
            for g in range(2):
                set_whole(tcur[g], g)
        wait_bytes(hbuf.at[outer, pl.ds(0, nchip - 1)], h_recv.at[outer])
        s = add_up(hbuf.at[outer], range(nchip), send)
        dest_w = spread_group(s[:1], copies - 1) * (1.0 / (total_cols * nz))
        growth = chour[0] * (unpack_hour(s) * (1.0 / (total_rows * total_cols))) / dest_w
        cbuf[outer, 0] = growth
        remote(cbuf.at[outer, 0], cbuf.at[outer, 1], c_sem.at[0, outer], c_sem.at[1, outer], partner).start()
        pmine = hour_phi(growth, lambda: None)
        send = pack_tight(pmine)
        gmine[outer] = send
        start(gmine.at[outer], gbuf.at[outer], g_send.at[outer], g_recv.at[outer], everyone, chip, nchip)
        if outer == OUTER - 1:
            anchor_out[...] = uown[:, :rank]
            at = iota((piece, ncol), 1)
            at = (at // half + core) % 2 * half + at % half
            place = (at == me_orig * piece + iota((piece, ncol), 0)).astype(F32)
            d = jnp.concatenate(tcur, axis=1) / to_column(dest_w)
            dest_out[...] = lax.dot_general(place, d, (((1,), (1,)), ((), ())), precision=HIGH)
        remote(cbuf.at[outer, 0], cbuf.at[outer, 1], c_sem.at[0, outer], c_sem.at[1, outer], partner).wait_recv()
        wait_bytes(gbuf.at[outer, pl.ds(0, 2 * nchip - 1)], g_recv.at[outer])
        chour = [
            c * (unpack_tight(add_up(gbuf.at[outer], range(q * nchip, (q + 1) * nchip), (send, None)[q]))
                 * (1.0 / (total_rows * total_cols)))
            for q, c in enumerate((growth, cbuf[outer, 1]))]
        w = jnp.sum(chour[0] + chour[1], axis=0, keepdims=True) * (1.0 / nhour)
        chour = [c / w for c in chour]
        hour = jnp.concatenate([jnp.where(core == k, chour[0], chour[1]) for k in range(2)], axis=0)
        if outer < OUTER - 1:
            set_hours(hour / dest_w)
            uown[...] = uown[...] * w
            ufar[...] = ufar[...] * w

    hi = hour.astype(BF16).astype(F32)
    mid = (hour - hi).astype(BF16).astype(F32)
    terms = jnp.where(group == 0, hi, jnp.where(group == 1, mid, jnp.where(group == 2, hour - hi - mid, 0.0)))
    hour_out[...] = lax.dot_general(
        diag_all.astype(BF16), terms.astype(BF16), (((1,), (1,)), ((), ())), preferred_element_type=F32)
    weight_out[...] = w[:, :rank]

    wait_bytes(dbuf.at[pl.ds(0, norig - 1)], d_sem.at[0])
    acopy.wait_send()
    vcopy.wait_send()
    for e in range(OUTER * INNER * chunks):
        wait_bytes(ubuf.at[e, pl.ds(0, nx - 1)], u_send.at[e])
    for e in range(OUTER):
        wait_bytes(wbuf.at[e, pl.ds(0, nz - 1)], w_send.at[e])
        for k in range(2):
            wait_bytes(zbuf.at[2 * e + k, pl.ds(0, nz - 1)], z_send.at[2 * e + k])
        wait_bytes(tbuf.at[e, 0], t_sem.at[0, e])
        wait_bytes(cbuf.at[e, 0], c_sem.at[0, e])
        wait_bytes(hbuf.at[e, pl.ds(0, nchip - 1)], h_send.at[e])
        wait_bytes(gbuf.at[e, pl.ds(0, 2 * nchip - 1)], g_send.at[e])


def put_out(*refs):
    copies = [pltpu.make_async_copy(refs[q], refs[4 + q], refs[8].at[q]) for q in range(4)]
    for c in copies:
        c.start()
    for c in copies:
        c.wait()


def to_rows(row, rank):
    square = jnp.where(iota((rank, rank), 0) == iota((rank, rank), 1), jnp.broadcast_to(row, (rank, rank)), 0.0)
    return jnp.sum(square, axis=1, keepdims=True)


def on_device(counts, anchor_factor, dest_factor, hour_factor, weights):
    norig = lax.axis_size("orig")
    ndest = lax.axis_size("dest")
    nz, nx = norig // 2, 2 * ndest
    nchip = nz * ndest
    nrow, nhour, ncol = counts.shape
    rank = hour_factor.shape[1]
    khalf = nhour // 2
    chunks = nrow // 8
    hrow = -(-khalf // (8 * (LANES // rank - 1))) * 8
    prow = khalf * rank // LANES
    dma = pltpu.SemaphoreType.DMA
    vmem = pltpu.VMEM
    outs = pl.pallas_call(
        functools.partial(kernel, nz, ndest),
        out_shape=[
            jax.ShapeDtypeStruct(anchor_factor.shape, F32),
            jax.ShapeDtypeStruct(dest_factor.shape, F32),
            jax.ShapeDtypeStruct((rank, nhour), F32),
            jax.ShapeDtypeStruct((1, rank), F32),
        ],
        in_specs=[pl.BlockSpec(memory_space=pltpu.HBM)] * 5,
        out_specs=[pl.BlockSpec(memory_space=pltpu.VMEM)] * 4,
        scratch_shapes=[
            vmem((2, nrow, nhour, ncol), counts.dtype),
            vmem((chunks, 8 * nhour, ncol), F32),
            vmem((8 * nhour, LANES), F32),
            vmem((nrow, LANES), F32),
            vmem((nrow, LANES), F32),
            vmem((nhour, LANES), F32),
            vmem((2, 2 * LANES, 2 * LANES), BF16),
            vmem((2, 4 * rank, 2 * LANES), BF16),
            vmem((LANES, ncol), BF16),
            vmem((LANES, ncol), BF16),
            vmem((nrow * nhour, 2 * LANES), BF16),
            vmem((OUTER * INNER * chunks, 8, LANES), F32),
            vmem((OUTER * INNER * chunks, nx, 8, LANES), F32),
            vmem((OUTER, 8, LANES), F32),
            vmem((OUTER, nz, 8, LANES), F32),
            vmem((OUTER * 2, rank, LANES), F32),
            vmem((OUTER * 2, nz, rank, LANES), F32),
            vmem((OUTER, hrow, LANES), F32),
            vmem((OUTER, nchip, hrow, LANES), F32),
            vmem((OUTER, prow, LANES), F32),
            vmem((OUTER, 2 * nchip, prow, LANES), F32),
            vmem((2, nrow, LANES), F32),
            vmem((OUTER, 2, rank, LANES), F32),
            vmem((OUTER, 2, khalf, LANES), F32),
            vmem((norig,) + dest_factor.shape, F32),
            vmem(anchor_factor.shape, F32),
            vmem((rank, nhour), F32),
            vmem((1, rank), F32),
            dma((OUTER * INNER * chunks,)), dma((OUTER * INNER * chunks,)),
            dma((OUTER,)), dma((OUTER,)),
            dma((OUTER * 2,)), dma((OUTER * 2,)),
            dma((OUTER,)), dma((OUTER,)),
            dma((OUTER,)), dma((OUTER,)),
            dma((2, OUTER)), dma((2, OUTER)), dma((2,)), dma((2,)), dma((2,)), dma((4 + chunks,)),
        ],
        compiler_params=pltpu.CompilerParams(
            collective_id=0, has_side_effects=True, vmem_limit_bytes=67043328),
    )(counts, anchor_factor, dest_factor, hour_factor.T, weights.reshape(1, rank))
    outs = pl.pallas_call(
        put_out,
        out_shape=[jax.ShapeDtypeStruct(o.shape, F32) for o in outs],
        in_specs=[pl.BlockSpec(memory_space=pltpu.VMEM)] * 4,
        out_specs=[pl.BlockSpec(memory_space=pltpu.HBM)] * 4,
        scratch_shapes=[dma((4,))],
    )(*outs)
    return outs[0], outs[1], outs[2].T, outs[3].reshape(rank)


def solution(mesh):
    return jax.shard_map(
        on_device,
        mesh=mesh,
        in_specs=(P("orig", None, "dest"), P("orig", None), P(("dest", "orig"), None), P(), P()),
        out_specs=(P("orig", None), P(("dest", "orig"), None), P(), P()),
        check_vma=False,
    )
```

```python
import functools

import jax
import jax.numpy as jnp
from jax import lax
from jax.experimental import pallas as pl
from jax.experimental.pallas import tpu as pltpu
from jax.sharding import PartitionSpec as P

INNER = 2
OUTER = 2
LANES = 128
F32 = jnp.float32
BF16 = jnp.bfloat16
HIGH = lax.Precision.HIGHEST
MESH = pl.DeviceIdType.MESH


def iota(shape, dim):
    return lax.broadcasted_iota(jnp.int32, shape, dim)


def kernel(nz, ndest, counts_in, anchor_in, dest_in, hour_in, weight_in,
           anchor_out, dest_out, hour_out, weight_out,
           cnts, avals, cexp, uown, ufar, ccur, bmod, balo, tmod, talo, khbuf,
           umine, ubuf, wmine, wbuf, zmine, zbuf, hmine, hbuf, gmine, gbuf, abuf, tbuf, cbuf, dbuf,
           anchor_ref, hour_ref, weight_ref,
           u_send, u_recv, w_send, w_recv, z_send, z_recv, h_send, h_recv, g_send, g_recv, t_sem, c_sem, d_sem, a_sem, v_sem, in_sem):
    _, nrow, nhour, ncol = cnts.shape
    rank = hour_ref.shape[0]
    piece = dbuf.shape[1]
    copies = LANES // rank
    half = ncol // 2
    khalf = nhour // 2
    nx = 2 * ndest
    norig = 2 * nz
    nchip = nz * ndest
    total_rows = nrow * norig
    total_cols = ncol * ndest
    me_orig = lax.axis_index("orig")
    me_dest = lax.axis_index("dest")
    zi = me_orig // 2
    core = me_orig % 2
    other = 1 - core
    chip = zi * ndest + me_dest
    partner = {"orig": zi * 2 + other}
    chunks = nrow // 8

    up = zi * 2 // nz
    own_place = (nz - 1 - zi) * (1 - up) + zi * up
    zline = []
    for t in range(nz - 1):
        place = t + (t - own_place + nz) // nz
        zline.append((nz - 1 - place) * (1 - up) + place * up)
    zline.append(zi)
    side = 1 - 2 * (me_dest % 2)
    if ndest == 4:
        plane = [3 - me_dest, me_dest + side, (me_dest + 2) % 4, me_dest]
    else:
        plane = [(me_dest + t) % ndest for t in range(1, ndest)] + [me_dest]
    xpeers = [({"orig": zi * 2 + c, "dest": d}, k) for d in plane for k, c in enumerate((core, other))]
    xpeers = xpeers[:-2] + xpeers[-1:]
    zpeers = [({"orig": z * 2 + core}, 0) for z in zline[:-1]]
    opeers = [{"orig": z * 2 + c} for z in zline for c in (core, other)]
    opeers = opeers[:-2] + opeers[-1:]
    everyone = [({"orig": z * 2 + c, "dest": d}, k) for z in zline for d in plane for k, c in enumerate((core, other))]
    everyone = everyone[:-2] + everyone[-1:]
    cpeers = [who for who in everyone if who[1] == 0]

    small = [pltpu.make_async_copy(a, b, in_sem.at[q]) for q, (a, b) in enumerate(
        ((anchor_in, anchor_ref), (dest_in, dbuf.at[me_orig]), (hour_in, hour_ref), (weight_in, weight_ref)))]
    large = [pltpu.make_async_copy(counts_in.at[pl.ds(8 * s, 8)], cnts.at[0, pl.ds(8 * s, 8)], in_sem.at[4 + s])
             for s in range(chunks)]
    for dma in small + large:
        dma.start()
    barrier = pltpu.get_barrier_semaphore()
    near = opeers[:-1] + [who for who, _ in xpeers]
    for who in near:
        pl.semaphore_signal(barrier, inc=1, device_id=who, device_id_type=MESH)

    def remote(src, dst, send, recv, who):
        return pltpu.make_async_remote_copy(
            src_ref=src, dst_ref=dst, send_sem=send, recv_sem=recv, device_id=who, device_id_type=MESH)

    def start(mine, ref, send, recv, peers, slot, n):
        for who, far in peers:
            remote(mine, ref.at[slot + n * far], send, recv, who).start()

    def wait_bytes(ref, sem):
        pltpu.make_async_copy(ref, ref, sem).wait()

    def add_up(ref, slots, total):
        parts = [ref[s] for s in slots] + ([] if total is None else [total])
        while len(parts) > 1:
            parts = [a + b for a, b in zip(parts[::2], parts[1::2])] + parts[len(parts) // 2 * 2:]
        return parts[0]

    lane = iota((1, LANES), 1)
    group = lane // rank
    spread = (iota((rank, LANES), 1) % rank == iota((rank, LANES), 0)).astype(F32)
    diag = iota((rank, LANES), 1) == iota((rank, LANES), 0)
    diag_all = iota((rank, LANES), 1) % rank == iota((rank, LANES), 0)

    def to_column(row):
        return jnp.sum(jnp.where(diag, jnp.broadcast_to(row, (rank, LANES)), 0.0), axis=1, keepdims=True)

    def to_row(column):
        return jnp.sum(jnp.where(diag_all, jnp.broadcast_to(column, (rank, LANES)), 0.0), axis=0, keepdims=True)

    def sum_groups(x):
        step = rank
        while step < LANES:
            x = x + pltpu.roll(x, step, 1)
            step *= 2
        return x

    def spread_group(x, b):
        return sum_groups(jnp.where(group == b, x, 0.0))

    def pair_up(x):
        return x + pltpu.roll(x, rank, 1)

    def twice(x):
        return jnp.concatenate([x, x], axis=1)

    hrow = hbuf.shape[2]
    prow = gbuf.shape[2]
    hblocks = khalf // hrow

    def pack_hour(p, extra):
        out = jnp.broadcast_to(extra, (hrow, LANES))
        for b in range(hblocks):
            out = jnp.where(group == b, p[b * hrow:(b + 1) * hrow], out)
        return out

    def unpack_hour(s):
        return jnp.concatenate([spread_group(s, b) for b in range(hblocks)], axis=0)

    def pack_tight(p):
        out = p[:prow]
        for b in range(1, copies):
            out = jnp.where(group == b, p[b * prow:(b + 1) * prow], out)
        return out

    def unpack_tight(s):
        return jnp.concatenate([spread_group(s, b) for b in range(copies)], axis=0)

    def set_hours(c):
        ccur[...] = c
        cexp[...] = jnp.broadcast_to(c[:, None, :], (nhour, 8, LANES)).reshape(8 * nhour, LANES)

    for dma in (small[0], small[2], small[3]):
        dma.wait()
    weight_row = jnp.sum(jnp.where(
        diag_all, jnp.broadcast_to(to_rows(weight_ref[...], rank), (rank, LANES)), 0.0), axis=0, keepdims=True)
    own_anchor = lax.dot(anchor_ref[...], spread, precision=HIGH) * weight_row
    abuf[0] = own_anchor
    uown[...] = own_anchor
    set_hours(lax.dot_general(hour_ref[...], spread, (((0,), (0,)), ((), ())), precision=HIGH))
    bmod[...] = jnp.zeros_like(bmod)
    balo[...] = jnp.zeros_like(balo)
    for ref, slot in ((ubuf, me_dest), (wbuf, zi), (zbuf, zi), (hbuf, chip), (gbuf, chip)):
        for e in range(ref.shape[0]):
            ref[e, slot] = jnp.zeros(ref.shape[2:], F32)

    small[1].wait()
    pl.semaphore_wait(barrier, len(near))

    for who in opeers:
        remote(dbuf.at[me_orig], dbuf.at[me_orig], d_sem.at[0], d_sem.at[1], who).start()
    acopy = remote(abuf.at[0], abuf.at[1], a_sem.at[0], a_sem.at[1], partner)
    vcopy = remote(counts_in, cnts.at[1], v_sem.at[0], v_sem.at[1], partner)
    acopy.start()

    def split(t):
        hi = t.astype(BF16).astype(F32)
        return hi, t - hi

    def set_block(t, g):
        hi, lo = split(t)
        model = jnp.concatenate([hi] * (copies // 2) + [lo] * (copies // 2), axis=0).astype(BF16)
        for q in range(2):
            lanes = slice(q * LANES, (q + 1) * LANES)
            bmod[g, lanes, lanes] = model

    def set_along(t, g):
        along = jnp.concatenate(split(t), axis=0).astype(BF16)
        for q in range(2):
            balo[g, q * 2 * rank:(q + 1) * 2 * rank, q * LANES:(q + 1) * LANES] = along

    def set_whole(t, g):
        hi, lo = split(t)
        lanes = slice(g * half, (g + 1) * half)
        tmod[:, lanes] = jnp.concatenate([hi] * (copies // 2) + [lo] * (copies // 2), axis=0).astype(BF16)
        talo[:, lanes] = jnp.concatenate([hi, lo] * (copies // 2), axis=0).astype(BF16)

    high_lane = (iota((1, LANES), 1) // rank) % 2 == 0
    high_lanes = (iota((1, 2 * LANES), 1) // rank) % 2 == 0

    def split_low(kh, high):
        hi = kh.astype(BF16).astype(F32)
        return jnp.where(high, hi, kh - hi).astype(BF16)

    def block_kh(left, right):
        kh = (left[:, None, :] * right[None, :, :]).reshape(left.shape[0] * right.shape[0], 2 * LANES)
        return split_low(kh, high_lanes)

    def ratio_of(khs, values, right):
        model = jnp.dot(khs, right, preferred_element_type=F32)
        return (values / model).astype(BF16)

    def along_of(r, right):
        return lax.dot_general(r, right, (((1,), (1,)), ((), ())), preferred_element_type=F32)

    sides = [pl.ds(pl.multiple_of(c * half, half), half) for c in (core, other)]
    hours = pl.ds(pl.multiple_of(core * khalf, khalf), khalf)

    def block(s, hrs, g):
        return jnp.concatenate([
            cnts[q, 8 * s:8 * s + 8, hrs, sides[g]].reshape(-1, half).astype(F32) for q in range(2)], axis=1)

    def anchor_step(e, before):
        mine = []

        def finish(s, r):
            p = pair_up(jnp.sum((along_of(r, talo[...]) * cexp[...]).reshape(nhour, 8, LANES), axis=0))
            at = e * chunks + s
            umine[at] = p
            start(umine.at[at], ubuf.at[at], u_send.at[at], u_recv.at[at], xpeers, me_dest, ndest)
            mine.append(p)

        held = None
        for s in range(chunks):
            before(s)
            left = uown[8 * s:8 * s + 8]
            kh = (left[None] * cexp[...].reshape(nhour, 8, LANES)).reshape(8 * nhour, LANES)
            r = ratio_of(split_low(kh, high_lane), avals[s], tmod[...])
            if held is not None:
                finish(*held)
                held = None
            if e % INNER == 0 and s < chunks - 1:
                held = (s, r)
            else:
                finish(s, r)
        return mine

    def anchor_update(e, mine):
        def update(s):
            at = e * chunks + s
            if e == 0 and s == 0:
                acopy.wait_recv()
                ufar[...] = abuf[1]
            wait_bytes(ubuf.at[at, pl.ds(0, nx - 1)], u_recv.at[at])
            rows = slice(8 * s, 8 * s + 8)
            p = add_up(ubuf.at[at], range(ndest), mine[s])
            uown[rows] = uown[rows] * (p * (1.0 / (nhour * total_cols)))
            p = add_up(ubuf.at[at], range(ndest, nx), None)
            ufar[rows] = ufar[rows] * (p * (1.0 / (nhour * total_cols)))
        return update

    def both(s):
        rows = slice(8 * s, 8 * s + 8)
        return jnp.concatenate([uown[rows], ufar[rows]], axis=1)

    def dest_phi(before, inner):
        crow = 8 * nhour
        right = twice(ccur[...])
        total = None
        held = None

        def add(khs, r, total):
            for q in range(2):
                lanes = slice(q * LANES, (q + 1) * LANES)
                part = lax.dot_general(
                    khs[:, lanes], r[:, lanes], (((0,), (0,)), ((), ())), preferred_element_type=F32)
                total = part if total is None else total + part
            return total

        for s in range(chunks):
            if inner == 0:
                before(s)
                khs = block_kh(both(s), right)
                khbuf[s * crow:(s + 1) * crow] = khs
            else:
                khs = khbuf[s * crow:(s + 1) * crow]
            r = ratio_of(khs, block(s, slice(None), 0), bmod[0])
            if held is not None:
                total = add(*held, total)
                held = None
            if inner and s < chunks - 1:
                held = (khs, r)
            else:
                total = add(khs, r, total)
        return total[:rank] + total[rank:2 * rank]

    def hour_phi(c, between):
        right = twice(c)
        crow = 8 * khalf
        p = None
        held = None

        def along(r, left, g, p):
            mixed = jnp.where(group < 2, left[:, :LANES], left[:, LANES:])
            part = jnp.sum(along_of(r, balo[g]).reshape(8, khalf, LANES) * mixed[:, None, :], axis=0)
            return part if p is None else p + part

        for g in range(2):
            if g:
                between()
            for s in range(chunks):
                left = both(s)
                if g == 0:
                    khs = block_kh(left, right)
                    khbuf[s * crow:(s + 1) * crow] = khs
                else:
                    khs = khbuf[s * crow:(s + 1) * crow]
                r = ratio_of(khs, block(s, hours, g), bmod[g])
                if held is not None:
                    p = along(*held, p)
                held = (r, left, g)
        return sum_groups(along(*held, p))

    def hour_phi_whole(c):
        p = None
        held = None

        def along(r, left, p):
            part = jnp.sum(along_of(r, talo[...]).reshape(8, khalf, LANES) * left[:, None, :], axis=0)
            return part if p is None else p + part

        for q, u in enumerate((uown, ufar)):
            for s in range(chunks):
                left = u[8 * s:8 * s + 8]
                khs = split_low((left[:, None, :] * c[None]).reshape(8 * khalf, LANES), high_lane)
                values = jnp.concatenate([
                    cnts[q, 8 * s:8 * s + 8, hours, sides[g]].reshape(-1, half).astype(F32) for g in range(2)], axis=1)
                r = ratio_of(khs, values, tmod[...])
                if held is not None:
                    p = along(*held, p)
                held = (r, left)
        return pair_up(along(*held, p))

    for s in range(chunks):
        large[s].wait()
        for g in range(2):
            v = cnts[0, 8 * s:8 * s + 8, :, sides[g]].astype(F32)
            avals[s, :, g * half:(g + 1) * half] = jnp.swapaxes(v, 0, 1).reshape(8 * nhour, half)

    wait_bytes(dbuf.at[pl.ds(0, norig - 1)], d_sem.at[1])
    tcur = []
    for g, c in enumerate((core, other)):
        d = dbuf[pl.ds(c * nz, nz)].reshape(half, rank)
        tcur.append(jnp.transpose(d))
        set_whole(tcur[g], g)

    dest_w = None
    chour = None
    for outer in range(OUTER):
        before = lambda s: None
        for inner in range(INNER):
            mine = anchor_step(outer * INNER + inner, before)
            before = anchor_update(outer * INNER + inner, mine)
            if outer + inner == 0:
                vcopy.start()
            if inner == 0:
                set_block(tcur[0], 0)
                if chour is None:
                    chour = [jnp.where(core == k, ccur[:khalf], ccur[khalf:]) for k in range(2)]
        if outer == 0:
            vcopy.wait_recv()

        def settle(s):
            before(s)
            if s == chunks - 1:
                col = jnp.broadcast_to(jnp.sum(uown[...] + ufar[...], axis=0, keepdims=True), (8, LANES))
                wmine[outer] = col
                start(wmine.at[outer], wbuf.at[outer], w_send.at[outer], w_recv.at[outer], zpeers, zi, 0)

        for inner in range(INNER):
            e = outer * 2 + inner
            p = dest_phi(settle, inner)
            zmine[e] = p
            start(zmine.at[e], zbuf.at[e], z_send.at[e], z_recv.at[e], zpeers, zi, 0)
            if inner == 0:
                wait_bytes(wbuf.at[outer, pl.ds(0, nz - 1)], w_recv.at[outer])
                inv = (1.0 * total_rows) / add_up(wbuf.at[outer], range(nz), wmine[outer])[:1]
                old = tcur[0] * (to_column(inv if dest_w is None else inv * dest_w) * (1.0 / (total_rows * nhour)))
            else:
                old = tcur[0] * (1.0 / (total_rows * nhour))
                uown[...] = uown[...] * inv
                ufar[...] = ufar[...] * inv
            wait_bytes(zbuf.at[e, pl.ds(0, nz - 1)], z_recv.at[e])
            growth = old * add_up(zbuf.at[e], range(nz), p)
            if inner:
                tbuf[outer, 0] = growth
                remote(tbuf.at[outer, 0], tbuf.at[outer, 1], t_sem.at[0, outer], t_sem.at[1, outer], partner).start()
                set_along(growth, 0)
            tcur[0] = growth
            set_block(growth, 0)

        def far():
            remote(tbuf.at[outer, 0], tbuf.at[outer, 1], t_sem.at[0, outer], t_sem.at[1, outer], partner).wait_recv()
            tcur[1] = tbuf[outer, 1]
            set_block(tcur[1], 1)
            set_along(tcur[1], 1)

        pmine = hour_phi(chour[0], far)
        dest_col = to_row(jnp.sum(tcur[0] + tcur[1], axis=1, keepdims=True))
        send = pack_hour(pmine, dest_col)
        hmine[outer] = send
        start(hmine.at[outer], hbuf.at[outer], h_send.at[outer], h_recv.at[outer], cpeers, chip, 0)
        for g in range(2):
            set_whole(tcur[g], g)
        wait_bytes(hbuf.at[outer, pl.ds(0, nchip - 1)], h_recv.at[outer])
        s = add_up(hbuf.at[outer], range(nchip), send)
        dest_w = spread_group(s[:1], copies - 1) * (1.0 / (total_cols * nz))
        growth = (chour[0] * unpack_hour(s)) * ((1.0 / (total_rows * total_cols)) / dest_w)
        cbuf[outer, 0] = growth
        remote(cbuf.at[outer, 0], cbuf.at[outer, 1], c_sem.at[0, outer], c_sem.at[1, outer], partner).start()
        pmine = hour_phi_whole(growth)
        send = pack_tight(pmine)
        gmine[outer] = send
        start(gmine.at[outer], gbuf.at[outer], g_send.at[outer], g_recv.at[outer], everyone, chip, nchip)
        if outer == OUTER - 1:
            anchor_out[...] = uown[:, :rank]
            at = iota((piece, ncol), 1)
            at = (at // half + core) % 2 * half + at % half
            place = (at == me_orig * piece + iota((piece, ncol), 0)).astype(F32)
            d = jnp.concatenate(tcur, axis=1) / to_column(dest_w)
            dest_out[...] = lax.dot_general(place, d, (((1,), (1,)), ((), ())), precision=HIGH)
            wait_bytes(dbuf.at[pl.ds(0, norig - 1)], d_sem.at[0])
            acopy.wait_send()
            vcopy.wait_send()
            for e in range(OUTER * INNER * chunks):
                wait_bytes(ubuf.at[e, pl.ds(0, nx - 1)], u_send.at[e])
            for e in range(OUTER):
                wait_bytes(wbuf.at[e, pl.ds(0, nz - 1)], w_send.at[e])
                for k in range(2):
                    wait_bytes(zbuf.at[2 * e + k, pl.ds(0, nz - 1)], z_send.at[2 * e + k])
                wait_bytes(tbuf.at[e, 0], t_sem.at[0, e])
                wait_bytes(cbuf.at[e, 0], c_sem.at[0, e])
                wait_bytes(hbuf.at[e, pl.ds(0, nchip - 1)], h_send.at[e])
            for e in range(OUTER - 1):
                wait_bytes(gbuf.at[e, pl.ds(0, 2 * nchip - 1)], g_send.at[e])
        remote(cbuf.at[outer, 0], cbuf.at[outer, 1], c_sem.at[0, outer], c_sem.at[1, outer], partner).wait_recv()
        wait_bytes(gbuf.at[outer, pl.ds(0, 2 * nchip - 1)], g_recv.at[outer])
        chour = [
            c * (unpack_tight(add_up(gbuf.at[outer], range(q * nchip, (q + 1) * nchip), (send, None)[q]))
                 * (1.0 / (total_rows * total_cols)))
            for q, c in enumerate((growth, cbuf[outer, 1]))]
        w = jnp.sum(chour[0] + chour[1], axis=0, keepdims=True) * (1.0 / nhour)
        chour = [c / w for c in chour]
        hour = jnp.concatenate([jnp.where(core == k, chour[0], chour[1]) for k in range(2)], axis=0)
        if outer < OUTER - 1:
            set_hours(hour / dest_w)
            uown[...] = uown[...] * w
            ufar[...] = ufar[...] * w

    hi = hour.astype(BF16).astype(F32)
    mid = (hour - hi).astype(BF16).astype(F32)
    terms = jnp.where(group == 0, hi, jnp.where(group == 1, mid, jnp.where(group == 2, hour - hi - mid, 0.0)))
    hour_out[...] = lax.dot_general(
        diag_all.astype(BF16), terms.astype(BF16), (((1,), (1,)), ((), ())), preferred_element_type=F32)
    weight_out[...] = w[:, :rank]

    wait_bytes(gbuf.at[OUTER - 1, pl.ds(0, 2 * nchip - 1)], g_send.at[OUTER - 1])


def put_out(*refs):
    copies = [pltpu.make_async_copy(refs[q], refs[4 + q], refs[8].at[q]) for q in range(4)]
    for c in copies:
        c.start()
    for c in copies:
        c.wait()


def to_rows(row, rank):
    square = jnp.where(iota((rank, rank), 0) == iota((rank, rank), 1), jnp.broadcast_to(row, (rank, rank)), 0.0)
    return jnp.sum(square, axis=1, keepdims=True)


def on_device(counts, anchor_factor, dest_factor, hour_factor, weights):
    norig = lax.axis_size("orig")
    ndest = lax.axis_size("dest")
    nz, nx = norig // 2, 2 * ndest
    nchip = nz * ndest
    nrow, nhour, ncol = counts.shape
    rank = hour_factor.shape[1]
    khalf = nhour // 2
    chunks = nrow // 8
    hrow = -(-khalf // (8 * (LANES // rank - 1))) * 8
    prow = khalf * rank // LANES
    dma = pltpu.SemaphoreType.DMA
    vmem = pltpu.VMEM
    outs = pl.pallas_call(
        functools.partial(kernel, nz, ndest),
        out_shape=[
            jax.ShapeDtypeStruct(anchor_factor.shape, F32),
            jax.ShapeDtypeStruct(dest_factor.shape, F32),
            jax.ShapeDtypeStruct((rank, nhour), F32),
            jax.ShapeDtypeStruct((1, rank), F32),
        ],
        in_specs=[pl.BlockSpec(memory_space=pltpu.HBM)] * 5,
        out_specs=[pl.BlockSpec(memory_space=pltpu.VMEM)] * 4,
        scratch_shapes=[
            vmem((2, nrow, nhour, ncol), counts.dtype),
            vmem((chunks, 8 * nhour, ncol), F32),
            vmem((8 * nhour, LANES), F32),
            vmem((nrow, LANES), F32),
            vmem((nrow, LANES), F32),
            vmem((nhour, LANES), F32),
            vmem((2, 2 * LANES, 2 * LANES), BF16),
            vmem((2, 4 * rank, 2 * LANES), BF16),
            vmem((LANES, ncol), BF16),
            vmem((LANES, ncol), BF16),
            vmem((nrow * nhour, 2 * LANES), BF16),
            vmem((OUTER * INNER * chunks, 8, LANES), F32),
            vmem((OUTER * INNER * chunks, nx, 8, LANES), F32),
            vmem((OUTER, 8, LANES), F32),
            vmem((OUTER, nz, 8, LANES), F32),
            vmem((OUTER * 2, rank, LANES), F32),
            vmem((OUTER * 2, nz, rank, LANES), F32),
            vmem((OUTER, hrow, LANES), F32),
            vmem((OUTER, nchip, hrow, LANES), F32),
            vmem((OUTER, prow, LANES), F32),
            vmem((OUTER, 2 * nchip, prow, LANES), F32),
            vmem((2, nrow, LANES), F32),
            vmem((OUTER, 2, rank, LANES), F32),
            vmem((OUTER, 2, khalf, LANES), F32),
            vmem((norig,) + dest_factor.shape, F32),
            vmem(anchor_factor.shape, F32),
            vmem((rank, nhour), F32),
            vmem((1, rank), F32),
            dma((OUTER * INNER * chunks,)), dma((OUTER * INNER * chunks,)),
            dma((OUTER,)), dma((OUTER,)),
            dma((OUTER * 2,)), dma((OUTER * 2,)),
            dma((OUTER,)), dma((OUTER,)),
            dma((OUTER,)), dma((OUTER,)),
            dma((2, OUTER)), dma((2, OUTER)), dma((2,)), dma((2,)), dma((2,)), dma((4 + chunks,)),
        ],
        compiler_params=pltpu.CompilerParams(
            collective_id=0, has_side_effects=True, vmem_limit_bytes=67043328),
    )(counts, anchor_factor, dest_factor, hour_factor.T, weights.reshape(1, rank))
    outs = pl.pallas_call(
        put_out,
        out_shape=[jax.ShapeDtypeStruct(o.shape, F32) for o in outs],
        in_specs=[pl.BlockSpec(memory_space=pltpu.VMEM)] * 4,
        out_specs=[pl.BlockSpec(memory_space=pltpu.HBM)] * 4,
        scratch_shapes=[dma((4,))],
    )(*outs)
    return outs[0], outs[1], outs[2].T, outs[3].reshape(rank)


def solution(mesh):
    return jax.shard_map(
        on_device,
        mesh=mesh,
        in_specs=(P("orig", None, "dest"), P("orig", None), P(("dest", "orig"), None), P(), P()),
        out_specs=(P("orig", None), P(("dest", "orig"), None), P(), P()),
        check_vma=False,
    )
```

```python
import functools

import jax
import jax.numpy as jnp
from jax import lax
from jax.experimental import pallas as pl
from jax.experimental.pallas import tpu as pltpu
from jax.sharding import PartitionSpec as P

INNER = 2
OUTER = 2
LANES = 128
F32 = jnp.float32
BF16 = jnp.bfloat16
HIGH = lax.Precision.HIGHEST
MESH = pl.DeviceIdType.MESH


def iota(shape, dim):
    return lax.broadcasted_iota(jnp.int32, shape, dim)


def kernel(nz, ndest, counts_in, anchor_in, dest_in, hour_in, weight_in,
           anchor_out, dest_out, hour_out, weight_out,
           cnts, avals, cexp, uown, ufar, ccur, bmod, balo, tmod, talo, khbuf,
           umine, ubuf, wmine, wbuf, zmine, zbuf, hmine, hbuf, gmine, gbuf, abuf, tbuf, cbuf, dbuf,
           anchor_ref, hour_ref, weight_ref,
           u_send, u_recv, w_send, w_recv, z_send, z_recv, h_send, h_recv, g_send, g_recv, t_sem, c_sem, d_sem, a_sem, v_sem, in_sem):
    _, nrow, nhour, ncol = cnts.shape
    rank = hour_ref.shape[0]
    piece = dbuf.shape[1]
    copies = LANES // rank
    half = ncol // 2
    khalf = nhour // 2
    nx = 2 * ndest
    norig = 2 * nz
    nchip = nz * ndest
    total_rows = nrow * norig
    total_cols = ncol * ndest
    me_orig = lax.axis_index("orig")
    me_dest = lax.axis_index("dest")
    zi = me_orig // 2
    core = me_orig % 2
    other = 1 - core
    chip = zi * ndest + me_dest
    partner = {"orig": zi * 2 + other}
    chunks = nrow // 8

    up = zi * 2 // nz
    own_place = (nz - 1 - zi) * (1 - up) + zi * up
    zline = []
    for t in range(nz - 1):
        place = t + (t - own_place + nz) // nz
        zline.append((nz - 1 - place) * (1 - up) + place * up)
    zline.append(zi)
    side = 1 - 2 * (me_dest % 2)
    if ndest == 4:
        plane = [3 - me_dest, me_dest + side, (me_dest + 2) % 4, me_dest]
    else:
        plane = [(me_dest + t) % ndest for t in range(1, ndest)] + [me_dest]
    xpeers = [({"orig": zi * 2 + c, "dest": d}, k) for d in plane for k, c in enumerate((core, other))]
    xpeers = xpeers[:-2] + xpeers[-1:]
    zpeers = [({"orig": z * 2 + core}, 0) for z in zline[:-1]]
    opeers = [{"orig": z * 2 + c} for z in zline for c in (core, other)]
    opeers = opeers[:-2] + opeers[-1:]
    everyone = [({"orig": z * 2 + c, "dest": d}, k) for z in zline for d in plane for k, c in enumerate((core, other))]
    everyone = everyone[:-2] + everyone[-1:]
    cpeers = [who for who in everyone if who[1] == 0]

    small = [pltpu.make_async_copy(a, b, in_sem.at[q]) for q, (a, b) in enumerate(
        ((anchor_in, anchor_ref), (dest_in, dbuf.at[me_orig]), (hour_in, hour_ref), (weight_in, weight_ref)))]
    large = [pltpu.make_async_copy(counts_in.at[pl.ds(8 * s, 8)], cnts.at[0, pl.ds(8 * s, 8)], in_sem.at[4 + s])
             for s in range(chunks)]
    for dma in small + large:
        dma.start()
    barrier = pltpu.get_barrier_semaphore()
    near = opeers[:-1] + [who for who, _ in xpeers]
    for who in near:
        pl.semaphore_signal(barrier, inc=1, device_id=who, device_id_type=MESH)

    def remote(src, dst, send, recv, who):
        return pltpu.make_async_remote_copy(
            src_ref=src, dst_ref=dst, send_sem=send, recv_sem=recv, device_id=who, device_id_type=MESH)

    def start(mine, ref, send, recv, peers, slot, n):
        for who, far in peers:
            remote(mine, ref.at[slot + n * far], send, recv, who).start()

    def wait_bytes(ref, sem):
        pltpu.make_async_copy(ref, ref, sem).wait()

    def add_up(ref, slots, total):
        parts = [ref[s] for s in slots] + ([] if total is None else [total])
        while len(parts) > 1:
            parts = [a + b for a, b in zip(parts[::2], parts[1::2])] + parts[len(parts) // 2 * 2:]
        return parts[0]

    lane = iota((1, LANES), 1)
    group = lane // rank
    spread = (iota((rank, LANES), 1) % rank == iota((rank, LANES), 0)).astype(F32)
    diag = iota((rank, LANES), 1) == iota((rank, LANES), 0)
    diag_all = iota((rank, LANES), 1) % rank == iota((rank, LANES), 0)

    def to_column(row):
        return jnp.sum(jnp.where(diag, jnp.broadcast_to(row, (rank, LANES)), 0.0), axis=1, keepdims=True)

    def to_row(column):
        return jnp.sum(jnp.where(diag_all, jnp.broadcast_to(column, (rank, LANES)), 0.0), axis=0, keepdims=True)

    def sum_groups(x):
        step = rank
        while step < LANES:
            x = x + pltpu.roll(x, step, 1)
            step *= 2
        return x

    def spread_group(x, b):
        return sum_groups(jnp.where(group == b, x, 0.0))

    def pair_up(x):
        return x + pltpu.roll(x, rank, 1)

    def twice(x):
        return jnp.concatenate([x, x], axis=1)

    hrow = hbuf.shape[2]
    prow = gbuf.shape[2]
    hblocks = khalf // hrow

    def pack_hour(p, extra):
        out = jnp.broadcast_to(extra, (hrow, LANES))
        for b in range(hblocks):
            out = jnp.where(group == b, p[b * hrow:(b + 1) * hrow], out)
        return out

    def unpack_hour(s):
        return jnp.concatenate([spread_group(s, b) for b in range(hblocks)], axis=0)

    def pack_tight(p):
        out = p[:prow]
        for b in range(1, copies):
            out = jnp.where(group == b, p[b * prow:(b + 1) * prow], out)
        return out

    def unpack_tight(s):
        return jnp.concatenate([spread_group(s, b) for b in range(copies)], axis=0)

    def set_hours(c):
        ccur[...] = c
        cexp[...] = jnp.broadcast_to(c[:, None, :], (nhour, 8, LANES)).reshape(8 * nhour, LANES)

    for dma in (small[0], small[2], small[3]):
        dma.wait()
    weight_row = jnp.sum(jnp.where(
        diag_all, jnp.broadcast_to(to_rows(weight_ref[...], rank), (rank, LANES)), 0.0), axis=0, keepdims=True)
    own_anchor = lax.dot(anchor_ref[...], spread, precision=HIGH) * weight_row
    abuf[0] = own_anchor
    uown[...] = own_anchor
    set_hours(lax.dot_general(hour_ref[...], spread, (((0,), (0,)), ((), ())), precision=HIGH))
    balo[...] = jnp.zeros_like(balo)
    for ref, slot in ((ubuf, me_dest), (wbuf, zi), (zbuf, zi), (hbuf, chip), (gbuf, chip)):
        for e in range(ref.shape[0]):
            ref[e, slot] = jnp.zeros(ref.shape[2:], F32)

    small[1].wait()
    pl.semaphore_wait(barrier, len(near))

    for who in opeers:
        remote(dbuf.at[me_orig], dbuf.at[me_orig], d_sem.at[0], d_sem.at[1], who).start()
    acopy = remote(abuf.at[0], abuf.at[1], a_sem.at[0], a_sem.at[1], partner)
    vcopy = remote(counts_in, cnts.at[1], v_sem.at[0], v_sem.at[1], partner)
    acopy.start()

    def split(t):
        hi = t.astype(BF16).astype(F32)
        return hi, t - hi

    def set_block(t, g):
        hi, lo = split(t)
        bmod[g] = jnp.concatenate([hi] * (copies // 2) + [lo] * (copies // 2), axis=0).astype(BF16)

    def set_along(t, g):
        along = jnp.concatenate(split(t), axis=0).astype(BF16)
        for q in range(2):
            balo[g, q * 2 * rank:(q + 1) * 2 * rank, q * LANES:(q + 1) * LANES] = along

    def set_whole(t, g):
        hi, lo = split(t)
        lanes = slice(g * half, (g + 1) * half)
        tmod[:, lanes] = jnp.concatenate([hi] * (copies // 2) + [lo] * (copies // 2), axis=0).astype(BF16)
        talo[:, lanes] = jnp.concatenate([hi, lo] * (copies // 2), axis=0).astype(BF16)

    high_lane = (iota((1, LANES), 1) // rank) % 2 == 0
    high_lanes = (iota((1, 2 * LANES), 1) // rank) % 2 == 0

    def split_low(kh, high):
        hi = kh.astype(BF16).astype(F32)
        return jnp.where(high, hi, kh - hi).astype(BF16)

    def block_kh(left, right):
        kh = (left[:, None, :] * right[None, :, :]).reshape(left.shape[0] * right.shape[0], 2 * LANES)
        return split_low(kh, high_lanes)

    def ratio_of(khs, values, right):
        if khs.shape[1] == 2 * LANES:
            model = jnp.concatenate([
                jnp.dot(khs[:, q * LANES:(q + 1) * LANES], right, preferred_element_type=F32) for q in range(2)], axis=1)
        else:
            model = jnp.dot(khs, right, preferred_element_type=F32)
        return (values / model).astype(BF16)

    def along_of(r, right):
        return lax.dot_general(r, right, (((1,), (1,)), ((), ())), preferred_element_type=F32)

    sides = [pl.ds(pl.multiple_of(c * half, half), half) for c in (core, other)]
    hours = pl.ds(pl.multiple_of(core * khalf, khalf), khalf)

    def block(s, hrs, g):
        return jnp.concatenate([
            cnts[q, 8 * s:8 * s + 8, hrs, sides[g]].reshape(-1, half).astype(F32) for q in range(2)], axis=1)

    def anchor_step(e, before):
        mine = []

        def finish(s, r):
            p = pair_up(jnp.sum((along_of(r, talo[...]) * cexp[...]).reshape(nhour, 8, LANES), axis=0))
            at = e * chunks + s
            umine[at] = p
            start(umine.at[at], ubuf.at[at], u_send.at[at], u_recv.at[at], xpeers, me_dest, ndest)
            mine.append(p)

        held = None
        for s in range(chunks):
            before(s)
            left = uown[8 * s:8 * s + 8]
            kh = (left[None] * cexp[...].reshape(nhour, 8, LANES)).reshape(8 * nhour, LANES)
            r = ratio_of(split_low(kh, high_lane), avals[s], tmod[...])
            if held is not None:
                finish(*held)
                held = None
            if e % INNER == 0 and s < chunks - 1:
                held = (s, r)
            else:
                finish(s, r)
        return mine

    def anchor_update(e, mine):
        def update(s):
            at = e * chunks + s
            if e == 0 and s == 0:
                acopy.wait_recv()
                ufar[...] = abuf[1]
            wait_bytes(ubuf.at[at, pl.ds(0, nx - 1)], u_recv.at[at])
            rows = slice(8 * s, 8 * s + 8)
            p = add_up(ubuf.at[at], range(ndest), mine[s])
            uown[rows] = uown[rows] * (p * (1.0 / (nhour * total_cols)))
            p = add_up(ubuf.at[at], range(ndest, nx), None)
            ufar[rows] = ufar[rows] * (p * (1.0 / (nhour * total_cols)))
        return update

    def both(s):
        rows = slice(8 * s, 8 * s + 8)
        return jnp.concatenate([uown[rows], ufar[rows]], axis=1)

    def dest_phi(before, inner):
        crow = 8 * nhour
        right = twice(ccur[...])
        total = None
        held = None

        def add(khs, r, total):
            part = lax.dot_general(
                jnp.concatenate([khs[:, :LANES], khs[:, LANES:]], axis=0),
                jnp.concatenate([r[:, :LANES], r[:, LANES:]], axis=0),
                (((0,), (0,)), ((), ())), preferred_element_type=F32)
            return part if total is None else total + part

        for s in range(chunks):
            if inner == 0:
                before(s)
                khs = block_kh(both(s), right)
                khbuf[s * crow:(s + 1) * crow] = khs
            else:
                khs = khbuf[s * crow:(s + 1) * crow]
            r = ratio_of(khs, block(s, slice(None), 0), bmod[0])
            if held is not None:
                total = add(*held, total)
                held = None
            if inner and s < chunks - 1:
                held = (khs, r)
            else:
                total = add(khs, r, total)
        return total[:rank] + total[rank:2 * rank]

    def hour_phi(c, between):
        right = twice(c)
        crow = 8 * khalf
        p = None
        held = None

        def along(r, left, g, p):
            mixed = jnp.where(group < 2, left[:, :LANES], left[:, LANES:])
            part = jnp.sum(along_of(r, balo[g]).reshape(8, khalf, LANES) * mixed[:, None, :], axis=0)
            return part if p is None else p + part

        for g in range(2):
            if g:
                between()
            for s in range(chunks):
                left = both(s)
                if g == 0:
                    khs = block_kh(left, right)
                    khbuf[s * crow:(s + 1) * crow] = khs
                else:
                    khs = khbuf[s * crow:(s + 1) * crow]
                r = ratio_of(khs, block(s, hours, g), bmod[g])
                if held is not None:
                    p = along(*held, p)
                held = (r, left, g)
        return sum_groups(along(*held, p))

    def hour_phi_whole(c):
        p = None
        held = None

        def along(r, left, p):
            part = jnp.sum(along_of(r, talo[...]).reshape(8, khalf, LANES) * left[:, None, :], axis=0)
            return part if p is None else p + part

        for q, u in enumerate((uown, ufar)):
            for s in range(chunks):
                left = u[8 * s:8 * s + 8]
                khs = split_low((left[:, None, :] * c[None]).reshape(8 * khalf, LANES), high_lane)
                values = jnp.concatenate([
                    cnts[q, 8 * s:8 * s + 8, hours, sides[g]].reshape(-1, half).astype(F32) for g in range(2)], axis=1)
                r = ratio_of(khs, values, tmod[...])
                if held is not None:
                    p = along(*held, p)
                held = (r, left)
        return pair_up(along(*held, p))

    for s in range(chunks):
        large[s].wait()
        for g in range(2):
            v = cnts[0, 8 * s:8 * s + 8, :, sides[g]].astype(F32)
            avals[s, :, g * half:(g + 1) * half] = jnp.swapaxes(v, 0, 1).reshape(8 * nhour, half)

    wait_bytes(dbuf.at[pl.ds(0, norig - 1)], d_sem.at[1])
    tcur = []
    for g, c in enumerate((core, other)):
        d = dbuf[pl.ds(c * nz, nz)].reshape(half, rank)
        tcur.append(jnp.transpose(d))
        set_whole(tcur[g], g)

    dest_w = None
    chour = None
    for outer in range(OUTER):
        before = lambda s: None
        for inner in range(INNER):
            mine = anchor_step(outer * INNER + inner, before)
            before = anchor_update(outer * INNER + inner, mine)
            if outer + inner == 0:
                vcopy.start()
            if inner == 0:
                set_block(tcur[0], 0)
                if chour is None:
                    chour = [jnp.where(core == k, ccur[:khalf], ccur[khalf:]) for k in range(2)]
        if outer == 0:
            vcopy.wait_recv()

        def settle(s):
            before(s)
            if s == chunks - 1:
                col = jnp.broadcast_to(jnp.sum(uown[...] + ufar[...], axis=0, keepdims=True), (8, LANES))
                wmine[outer] = col
                start(wmine.at[outer], wbuf.at[outer], w_send.at[outer], w_recv.at[outer], zpeers, zi, 0)

        for inner in range(INNER):
            e = outer * 2 + inner
            p = dest_phi(settle, inner)
            zmine[e] = p
            start(zmine.at[e], zbuf.at[e], z_send.at[e], z_recv.at[e], zpeers, zi, 0)
            if inner == 0:
                wait_bytes(wbuf.at[outer, pl.ds(0, nz - 1)], w_recv.at[outer])
                inv = (1.0 * total_rows) / add_up(wbuf.at[outer], range(nz), wmine[outer])[:1]
                old = tcur[0] * (to_column(inv if dest_w is None else inv * dest_w) * (1.0 / (total_rows * nhour)))
            else:
                old = tcur[0] * (1.0 / (total_rows * nhour))
                uown[...] = uown[...] * inv
                ufar[...] = ufar[...] * inv
            wait_bytes(zbuf.at[e, pl.ds(0, nz - 1)], z_recv.at[e])
            growth = old * add_up(zbuf.at[e], range(nz), p)
            if inner:
                tbuf[outer, 0] = growth
                remote(tbuf.at[outer, 0], tbuf.at[outer, 1], t_sem.at[0, outer], t_sem.at[1, outer], partner).start()
                set_along(growth, 0)
            tcur[0] = growth
            set_block(growth, 0)

        def far():
            remote(tbuf.at[outer, 0], tbuf.at[outer, 1], t_sem.at[0, outer], t_sem.at[1, outer], partner).wait_recv()
            tcur[1] = tbuf[outer, 1]
            set_block(tcur[1], 1)
            set_along(tcur[1], 1)

        pmine = hour_phi(chour[0], far)
        dest_col = to_row(jnp.sum(tcur[0] + tcur[1], axis=1, keepdims=True))
        send = pack_hour(pmine, dest_col)
        hmine[outer] = send
        start(hmine.at[outer], hbuf.at[outer], h_send.at[outer], h_recv.at[outer], cpeers, chip, 0)
        for g in range(2):
            set_whole(tcur[g], g)
        wait_bytes(hbuf.at[outer, pl.ds(0, nchip - 1)], h_recv.at[outer])
        s = add_up(hbuf.at[outer], range(nchip), send)
        dest_w = spread_group(s[:1], copies - 1) * (1.0 / (total_cols * nz))
        growth = (chour[0] * unpack_hour(s)) * ((1.0 / (total_rows * total_cols)) / dest_w)
        cbuf[outer, 0] = growth
        remote(cbuf.at[outer, 0], cbuf.at[outer, 1], c_sem.at[0, outer], c_sem.at[1, outer], partner).start()
        pmine = hour_phi_whole(growth)
        send = pack_tight(pmine)
        gmine[outer] = send
        start(gmine.at[outer], gbuf.at[outer], g_send.at[outer], g_recv.at[outer], everyone, chip, nchip)
        if outer == OUTER - 1:
            anchor_out[...] = uown[:, :rank]
            at = iota((piece, ncol), 1)
            at = (at // half + core) % 2 * half + at % half
            place = (at == me_orig * piece + iota((piece, ncol), 0)).astype(F32)
            d = jnp.concatenate(tcur, axis=1) / to_column(dest_w)
            dest_out[...] = lax.dot_general(place, d, (((1,), (1,)), ((), ())), precision=HIGH)
            wait_bytes(dbuf.at[pl.ds(0, norig - 1)], d_sem.at[0])
            acopy.wait_send()
            vcopy.wait_send()
            for e in range(OUTER * INNER * chunks):
                wait_bytes(ubuf.at[e, pl.ds(0, nx - 1)], u_send.at[e])
            for e in range(OUTER):
                wait_bytes(wbuf.at[e, pl.ds(0, nz - 1)], w_send.at[e])
                for k in range(2):
                    wait_bytes(zbuf.at[2 * e + k, pl.ds(0, nz - 1)], z_send.at[2 * e + k])
                wait_bytes(tbuf.at[e, 0], t_sem.at[0, e])
                wait_bytes(cbuf.at[e, 0], c_sem.at[0, e])
                wait_bytes(hbuf.at[e, pl.ds(0, nchip - 1)], h_send.at[e])
            for e in range(OUTER - 1):
                wait_bytes(gbuf.at[e, pl.ds(0, 2 * nchip - 1)], g_send.at[e])
        remote(cbuf.at[outer, 0], cbuf.at[outer, 1], c_sem.at[0, outer], c_sem.at[1, outer], partner).wait_recv()
        wait_bytes(gbuf.at[outer, pl.ds(0, 2 * nchip - 1)], g_recv.at[outer])
        chour = [
            c * (unpack_tight(add_up(gbuf.at[outer], range(q * nchip, (q + 1) * nchip), (send, None)[q]))
                 * (1.0 / (total_rows * total_cols)))
            for q, c in enumerate((growth, cbuf[outer, 1]))]
        w = jnp.sum(chour[0] + chour[1], axis=0, keepdims=True) * (1.0 / nhour)
        chour = [c / w for c in chour]
        hour = jnp.concatenate([jnp.where(core == k, chour[0], chour[1]) for k in range(2)], axis=0)
        if outer < OUTER - 1:
            set_hours(hour / dest_w)
            uown[...] = uown[...] * w
            ufar[...] = ufar[...] * w

    hi = hour.astype(BF16).astype(F32)
    mid = (hour - hi).astype(BF16).astype(F32)
    terms = jnp.where(group == 0, hi, jnp.where(group == 1, mid, jnp.where(group == 2, hour - hi - mid, 0.0)))
    hour_out[...] = lax.dot_general(
        diag_all.astype(BF16), terms.astype(BF16), (((1,), (1,)), ((), ())), preferred_element_type=F32)
    weight_out[...] = w[:, :rank]

    wait_bytes(gbuf.at[OUTER - 1, pl.ds(0, 2 * nchip - 1)], g_send.at[OUTER - 1])


def put_out(*refs):
    copies = [pltpu.make_async_copy(refs[q], refs[4 + q], refs[8].at[q]) for q in range(4)]
    for c in copies:
        c.start()
    for c in copies:
        c.wait()


def to_rows(row, rank):
    square = jnp.where(iota((rank, rank), 0) == iota((rank, rank), 1), jnp.broadcast_to(row, (rank, rank)), 0.0)
    return jnp.sum(square, axis=1, keepdims=True)


def on_device(counts, anchor_factor, dest_factor, hour_factor, weights):
    norig = lax.axis_size("orig")
    ndest = lax.axis_size("dest")
    nz, nx = norig // 2, 2 * ndest
    nchip = nz * ndest
    nrow, nhour, ncol = counts.shape
    rank = hour_factor.shape[1]
    khalf = nhour // 2
    chunks = nrow // 8
    hrow = -(-khalf // (8 * (LANES // rank - 1))) * 8
    prow = khalf * rank // LANES
    half = ncol // 2
    dma = pltpu.SemaphoreType.DMA
    vmem = pltpu.VMEM
    outs = pl.pallas_call(
        functools.partial(kernel, nz, ndest),
        out_shape=[
            jax.ShapeDtypeStruct(anchor_factor.shape, F32),
            jax.ShapeDtypeStruct(dest_factor.shape, F32),
            jax.ShapeDtypeStruct((rank, nhour), F32),
            jax.ShapeDtypeStruct((1, rank), F32),
        ],
        in_specs=[pl.BlockSpec(memory_space=pltpu.HBM)] * 5,
        out_specs=[pl.BlockSpec(memory_space=pltpu.VMEM)] * 4,
        scratch_shapes=[
            vmem((2, nrow, nhour, ncol), counts.dtype),
            vmem((chunks, 8 * nhour, ncol), F32),
            vmem((8 * nhour, LANES), F32),
            vmem((nrow, LANES), F32),
            vmem((nrow, LANES), F32),
            vmem((nhour, LANES), F32),
            vmem((2, LANES, half), BF16),
            vmem((2, 4 * rank, 2 * LANES), BF16),
            vmem((LANES, ncol), BF16),
            vmem((LANES, ncol), BF16),
            vmem((nrow * nhour, 2 * LANES), BF16),
            vmem((OUTER * INNER * chunks, 8, LANES), F32),
            vmem((OUTER * INNER * chunks, nx, 8, LANES), F32),
            vmem((OUTER, 8, LANES), F32),
            vmem((OUTER, nz, 8, LANES), F32),
            vmem((OUTER * 2, rank, LANES), F32),
            vmem((OUTER * 2, nz, rank, LANES), F32),
            vmem((OUTER, hrow, LANES), F32),
            vmem((OUTER, nchip, hrow, LANES), F32),
            vmem((OUTER, prow, LANES), F32),
            vmem((OUTER, 2 * nchip, prow, LANES), F32),
            vmem((2, nrow, LANES), F32),
            vmem((OUTER, 2, rank, LANES), F32),
            vmem((OUTER, 2, khalf, LANES), F32),
            vmem((norig,) + dest_factor.shape, F32),
            vmem(anchor_factor.shape, F32),
            vmem((rank, nhour), F32),
            vmem((1, rank), F32),
            dma((OUTER * INNER * chunks,)), dma((OUTER * INNER * chunks,)),
            dma((OUTER,)), dma((OUTER,)),
            dma((OUTER * 2,)), dma((OUTER * 2,)),
            dma((OUTER,)), dma((OUTER,)),
            dma((OUTER,)), dma((OUTER,)),
            dma((2, OUTER)), dma((2, OUTER)), dma((2,)), dma((2,)), dma((2,)), dma((4 + chunks,)),
        ],
        compiler_params=pltpu.CompilerParams(
            collective_id=0, has_side_effects=True, vmem_limit_bytes=67043328),
    )(counts, anchor_factor, dest_factor, hour_factor.T, weights.reshape(1, rank))
    outs = pl.pallas_call(
        put_out,
        out_shape=[jax.ShapeDtypeStruct(o.shape, F32) for o in outs],
        in_specs=[pl.BlockSpec(memory_space=pltpu.VMEM)] * 4,
        out_specs=[pl.BlockSpec(memory_space=pltpu.HBM)] * 4,
        scratch_shapes=[dma((4,))],
    )(*outs)
    return outs[0], outs[1], outs[2].T, outs[3].reshape(rank)


def solution(mesh):
    return jax.shard_map(
        on_device,
        mesh=mesh,
        in_specs=(P("orig", None, "dest"), P("orig", None), P(("dest", "orig"), None), P(), P()),
        out_specs=(P("orig", None), P(("dest", "orig"), None), P(), P()),
        check_vma=False,
    )
```

```python
import functools

import jax
import jax.numpy as jnp
from jax import lax
from jax.experimental import pallas as pl
from jax.experimental.pallas import tpu as pltpu
from jax.sharding import PartitionSpec as P

INNER = 2
OUTER = 2
LANES = 128
F32 = jnp.float32
BF16 = jnp.bfloat16
HIGH = lax.Precision.HIGHEST
MESH = pl.DeviceIdType.MESH


def iota(shape, dim):
    return lax.broadcasted_iota(jnp.int32, shape, dim)


def kernel(nz, ndest, counts_in, anchor_in, dest_in, hour_in, weight_in,
           anchor_out, dest_out, hour_out, weight_out,
           cnts, avals, cexp, uown, ufar, ccur, bmod, balo, tmod, talo, khbuf,
           umine, ubuf, wmine, wbuf, zmine, zbuf, hmine, hbuf, gmine, gbuf, abuf, tbuf, cbuf, dbuf,
           anchor_ref, hour_ref, weight_ref,
           u_send, u_recv, w_send, w_recv, z_send, z_recv, h_send, h_recv, g_send, g_recv, t_sem, c_sem, d_sem, a_sem, v_sem, in_sem):
    _, nrow, nhour, ncol = cnts.shape
    rank = hour_ref.shape[0]
    piece = dbuf.shape[1]
    copies = LANES // rank
    half = ncol // 2
    khalf = nhour // 2
    nx = 2 * ndest
    norig = 2 * nz
    nchip = nz * ndest
    total_rows = nrow * norig
    total_cols = ncol * ndest
    me_orig = lax.axis_index("orig")
    me_dest = lax.axis_index("dest")
    zi = me_orig // 2
    core = me_orig % 2
    other = 1 - core
    chip = zi * ndest + me_dest
    partner = {"orig": zi * 2 + other}
    chunks = nrow // 8

    up = zi * 2 // nz
    own_place = (nz - 1 - zi) * (1 - up) + zi * up
    zline = []
    for t in range(nz - 1):
        place = t + (t - own_place + nz) // nz
        zline.append((nz - 1 - place) * (1 - up) + place * up)
    zline.append(zi)
    side = 1 - 2 * (me_dest % 2)
    if ndest == 4:
        plane = [3 - me_dest, me_dest + side, (me_dest + 2) % 4, me_dest]
    else:
        plane = [(me_dest + t) % ndest for t in range(1, ndest)] + [me_dest]
    xpeers = [({"orig": zi * 2 + c, "dest": d}, k) for d in plane for k, c in enumerate((core, other))]
    xpeers = xpeers[:-2] + xpeers[-1:]
    zpeers = [({"orig": z * 2 + core}, 0) for z in zline[:-1]]
    opeers = [{"orig": z * 2 + c} for z in zline for c in (core, other)]
    opeers = opeers[:-2] + opeers[-1:]
    everyone = [({"orig": z * 2 + c, "dest": d}, k) for z in zline for d in plane for k, c in enumerate((core, other))]
    everyone = everyone[:-2] + everyone[-1:]
    cpeers = [who for who in everyone if who[1] == 0]
    everyone = cpeers + [who for who in everyone if who[1]]

    small = [pltpu.make_async_copy(a, b, in_sem.at[q]) for q, (a, b) in enumerate(
        ((anchor_in, anchor_ref), (dest_in, dbuf.at[me_orig]), (hour_in, hour_ref), (weight_in, weight_ref)))]
    large = [pltpu.make_async_copy(counts_in.at[pl.ds(8 * s, 8)], cnts.at[0, pl.ds(8 * s, 8)], in_sem.at[4 + s])
             for s in range(chunks)]
    for dma in small + large:
        dma.start()
    barrier = pltpu.get_barrier_semaphore()
    near = opeers[:-1] + [who for who, _ in xpeers]
    for who in near:
        pl.semaphore_signal(barrier, inc=1, device_id=who, device_id_type=MESH)

    def remote(src, dst, send, recv, who):
        return pltpu.make_async_remote_copy(
            src_ref=src, dst_ref=dst, send_sem=send, recv_sem=recv, device_id=who, device_id_type=MESH)

    def start(mine, ref, send, recv, peers, slot, n):
        for who, far in peers:
            remote(mine, ref.at[slot + n * far], send, recv, who).start()

    def wait_bytes(ref, sem):
        pltpu.make_async_copy(ref, ref, sem).wait()

    def add_up(ref, slots, total):
        parts = [ref[s] for s in slots] + ([] if total is None else [total])
        while len(parts) > 1:
            parts = [a + b for a, b in zip(parts[::2], parts[1::2])] + parts[len(parts) // 2 * 2:]
        return parts[0]

    lane = iota((1, LANES), 1)
    group = lane // rank
    spread = (iota((rank, LANES), 1) % rank == iota((rank, LANES), 0)).astype(F32)
    diag = iota((rank, LANES), 1) == iota((rank, LANES), 0)
    diag_all = iota((rank, LANES), 1) % rank == iota((rank, LANES), 0)

    def to_column(row):
        return jnp.sum(jnp.where(diag, jnp.broadcast_to(row, (rank, LANES)), 0.0), axis=1, keepdims=True)

    def to_row(column):
        return jnp.sum(jnp.where(diag_all, jnp.broadcast_to(column, (rank, LANES)), 0.0), axis=0, keepdims=True)

    def sum_groups(x):
        step = rank
        while step < LANES:
            x = x + pltpu.roll(x, step, 1)
            step *= 2
        return x

    def spread_group(x, b):
        return sum_groups(jnp.where(group == b, x, 0.0))

    def pair_up(x):
        return x + pltpu.roll(x, rank, 1)

    def twice(x):
        return jnp.concatenate([x, x], axis=1)

    hrow = hbuf.shape[2]
    prow = gbuf.shape[2]
    hblocks = khalf // hrow

    def pack_hour(p, extra):
        out = jnp.broadcast_to(extra, (hrow, LANES))
        for b in range(hblocks):
            out = jnp.where(group == b, p[b * hrow:(b + 1) * hrow], out)
        return out

    def unpack_hour(s):
        return jnp.concatenate([spread_group(s, b) for b in range(hblocks)], axis=0)

    def pack_tight(p):
        out = p[:prow]
        for b in range(1, copies):
            out = jnp.where(group == b, p[b * prow:(b + 1) * prow], out)
        return out

    def unpack_tight(s):
        return jnp.concatenate([spread_group(s, b) for b in range(copies)], axis=0)

    def set_hours(c):
        ccur[...] = c
        cexp[...] = jnp.broadcast_to(c[:, None, :], (nhour, 8, LANES)).reshape(8 * nhour, LANES)

    for dma in (small[0], small[2], small[3]):
        dma.wait()
    weight_row = jnp.sum(jnp.where(
        diag_all, jnp.broadcast_to(to_rows(weight_ref[...], rank), (rank, LANES)), 0.0), axis=0, keepdims=True)
    own_anchor = lax.dot(anchor_ref[...], spread, precision=HIGH) * weight_row
    abuf[0] = own_anchor
    uown[...] = own_anchor
    set_hours(lax.dot_general(hour_ref[...], spread, (((0,), (0,)), ((), ())), precision=HIGH))
    balo[...] = jnp.zeros_like(balo)
    for ref, slot in ((ubuf, me_dest), (wbuf, zi), (zbuf, zi), (hbuf, chip), (gbuf, chip)):
        for e in range(ref.shape[0]):
            ref[e, slot] = jnp.zeros(ref.shape[2:], F32)

    small[1].wait()
    pl.semaphore_wait(barrier, len(near))

    for who in opeers:
        remote(dbuf.at[me_orig], dbuf.at[me_orig], d_sem.at[0], d_sem.at[1], who).start()
    acopy = remote(abuf.at[0], abuf.at[1], a_sem.at[0], a_sem.at[1], partner)
    vcopy = remote(counts_in, cnts.at[1], v_sem.at[0], v_sem.at[1], partner)
    acopy.start()

    def split(t):
        hi = t.astype(BF16).astype(F32)
        return hi, t - hi

    def set_block(t, g):
        hi, lo = split(t)
        bmod[g] = jnp.concatenate([hi] * (copies // 2) + [lo] * (copies // 2), axis=0).astype(BF16)

    def set_along(t, g):
        along = jnp.concatenate(split(t), axis=0).astype(BF16)
        for q in range(2):
            balo[g, q * 2 * rank:(q + 1) * 2 * rank, q * LANES:(q + 1) * LANES] = along

    def set_whole(t, g):
        hi, lo = split(t)
        lanes = slice(g * half, (g + 1) * half)
        tmod[:, lanes] = jnp.concatenate([hi] * (copies // 2) + [lo] * (copies // 2), axis=0).astype(BF16)
        talo[:, lanes] = jnp.concatenate([hi, lo] * (copies // 2), axis=0).astype(BF16)

    high_lane = (iota((1, LANES), 1) // rank) % 2 == 0
    high_lanes = (iota((1, 2 * LANES), 1) // rank) % 2 == 0

    def split_low(kh, high):
        hi = kh.astype(BF16).astype(F32)
        return jnp.where(high, hi, kh - hi).astype(BF16)

    def block_kh(left, right):
        kh = (left[:, None, :] * right[None, :, :]).reshape(left.shape[0] * right.shape[0], 2 * LANES)
        return split_low(kh, high_lanes)

    def ratio_of(khs, values, right):
        if khs.shape[1] == 2 * LANES:
            model = jnp.concatenate([
                jnp.dot(khs[:, q * LANES:(q + 1) * LANES], right, preferred_element_type=F32) for q in range(2)], axis=1)
        else:
            model = jnp.dot(khs, right, preferred_element_type=F32)
        return (values / model).astype(BF16)

    def along_of(r, right):
        return lax.dot_general(r, right, (((1,), (1,)), ((), ())), preferred_element_type=F32)

    sides = [pl.ds(pl.multiple_of(c * half, half), half) for c in (core, other)]
    hours = pl.ds(pl.multiple_of(core * khalf, khalf), khalf)

    def block(s, hrs, g):
        return jnp.concatenate([
            cnts[q, 8 * s:8 * s + 8, hrs, sides[g]].reshape(-1, half).astype(F32) for q in range(2)], axis=1)

    def anchor_step(e, before):
        mine = []

        def finish(s, r):
            p = pair_up(jnp.sum((along_of(r, talo[...]) * cexp[...]).reshape(nhour, 8, LANES), axis=0))
            at = e * chunks + s
            umine[at] = p
            start(umine.at[at], ubuf.at[at], u_send.at[at], u_recv.at[at], xpeers, me_dest, ndest)
            mine.append(p)

        held = None
        for s in range(chunks):
            before(s)
            left = uown[8 * s:8 * s + 8]
            kh = (left[None] * cexp[...].reshape(nhour, 8, LANES)).reshape(8 * nhour, LANES)
            r = ratio_of(split_low(kh, high_lane), avals[s], tmod[...])
            if held is not None:
                finish(*held)
                held = None
            if e % INNER == 0 and s < chunks - 1:
                held = (s, r)
            else:
                finish(s, r)
        return mine

    def anchor_update(e, mine):
        def update(s):
            at = e * chunks + s
            if e == 0 and s == 0:
                acopy.wait_recv()
                ufar[...] = abuf[1]
            wait_bytes(ubuf.at[at, pl.ds(0, nx - 1)], u_recv.at[at])
            rows = slice(8 * s, 8 * s + 8)
            p = add_up(ubuf.at[at], range(ndest), mine[s])
            uown[rows] = uown[rows] * (p * (1.0 / (nhour * total_cols)))
            p = add_up(ubuf.at[at], range(ndest, nx), None)
            ufar[rows] = ufar[rows] * (p * (1.0 / (nhour * total_cols)))
        return update

    def both(s):
        rows = slice(8 * s, 8 * s + 8)
        return jnp.concatenate([uown[rows], ufar[rows]], axis=1)

    def dest_phi(before, inner):
        crow = 8 * nhour
        right = twice(ccur[...])
        total = None
        held = None

        def add(khs, r, total):
            part = lax.dot_general(
                jnp.concatenate([khs[:, :LANES], khs[:, LANES:]], axis=0),
                jnp.concatenate([r[:, :LANES], r[:, LANES:]], axis=0),
                (((0,), (0,)), ((), ())), preferred_element_type=F32)
            return part if total is None else total + part

        for s in range(chunks):
            if inner == 0:
                before(s)
                khs = block_kh(both(s), right)
                khbuf[s * crow:(s + 1) * crow] = khs
            else:
                khs = khbuf[s * crow:(s + 1) * crow]
            r = ratio_of(khs, block(s, slice(None), 0), bmod[0])
            if held is not None:
                total = add(*held, total)
                held = None
            if inner and s < chunks - 1:
                held = (khs, r)
            else:
                total = add(khs, r, total)
        return total[:rank] + total[rank:2 * rank]

    def hour_phi(c, between):
        right = twice(c)
        crow = 8 * khalf
        p = None
        held = None

        def along(r, left, g, p):
            mixed = jnp.where(group < 2, left[:, :LANES], left[:, LANES:])
            part = jnp.sum(along_of(r, balo[g]).reshape(8, khalf, LANES) * mixed[:, None, :], axis=0)
            return part if p is None else p + part

        for g in range(2):
            if g:
                between()
            for s in range(chunks):
                left = both(s)
                if g == 0:
                    khs = block_kh(left, right)
                    khbuf[s * crow:(s + 1) * crow] = khs
                else:
                    khs = khbuf[s * crow:(s + 1) * crow]
                r = ratio_of(khs, block(s, hours, g), bmod[g])
                if held is not None:
                    p = along(*held, p)
                held = (r, left, g)
        return sum_groups(along(*held, p))

    def hour_phi_whole(c):
        p = None
        held = None

        def along(r, left, p):
            part = jnp.sum(along_of(r, talo[...]).reshape(8, khalf, LANES) * left[:, None, :], axis=0)
            return part if p is None else p + part

        for q, u in enumerate((uown, ufar)):
            for s in range(chunks):
                left = u[8 * s:8 * s + 8]
                khs = split_low((left[:, None, :] * c[None]).reshape(8 * khalf, LANES), high_lane)
                values = jnp.concatenate([
                    cnts[q, 8 * s:8 * s + 8, hours, sides[g]].reshape(-1, half).astype(F32) for g in range(2)], axis=1)
                r = ratio_of(khs, values, tmod[...])
                if held is not None:
                    p = along(*held, p)
                held = (r, left)
        return pair_up(along(*held, p))

    for s in range(chunks):
        large[s].wait()
        for g in range(2):
            v = cnts[0, 8 * s:8 * s + 8, :, sides[g]].astype(F32)
            avals[s, :, g * half:(g + 1) * half] = jnp.swapaxes(v, 0, 1).reshape(8 * nhour, half)

    wait_bytes(dbuf.at[pl.ds(0, norig - 1)], d_sem.at[1])
    tcur = []
    for g, c in enumerate((core, other)):
        d = dbuf[pl.ds(c * nz, nz)].reshape(half, rank)
        tcur.append(jnp.transpose(d))
        set_whole(tcur[g], g)

    dest_w = None
    chour = None
    for outer in range(OUTER):
        before = lambda s: None
        for inner in range(INNER):
            mine = anchor_step(outer * INNER + inner, before)
            before = anchor_update(outer * INNER + inner, mine)
            if outer + inner == 0:
                vcopy.start()
            if inner == 0:
                set_block(tcur[0], 0)
                if chour is None:
                    chour = [jnp.where(core == k, ccur[:khalf], ccur[khalf:]) for k in range(2)]
        if outer == 0:
            vcopy.wait_recv()

        def settle(s):
            before(s)
            if s == chunks - 1:
                col = jnp.broadcast_to(jnp.sum(uown[...] + ufar[...], axis=0, keepdims=True), (8, LANES))
                wmine[outer] = col
                start(wmine.at[outer], wbuf.at[outer], w_send.at[outer], w_recv.at[outer], zpeers, zi, 0)

        for inner in range(INNER):
            e = outer * 2 + inner
            p = dest_phi(settle, inner)
            zmine[e] = p
            start(zmine.at[e], zbuf.at[e], z_send.at[e], z_recv.at[e], zpeers, zi, 0)
            if inner == 0:
                wait_bytes(wbuf.at[outer, pl.ds(0, nz - 1)], w_recv.at[outer])
                inv = (1.0 * total_rows) / add_up(wbuf.at[outer], range(nz), wmine[outer])[:1]
                old = tcur[0] * (to_column(inv if dest_w is None else inv * dest_w) * (1.0 / (total_rows * nhour)))
            else:
                old = tcur[0] * (1.0 / (total_rows * nhour))
                uown[...] = uown[...] * inv
                ufar[...] = ufar[...] * inv
            wait_bytes(zbuf.at[e, pl.ds(0, nz - 1)], z_recv.at[e])
            growth = old * add_up(zbuf.at[e], range(nz), p)
            if inner:
                tbuf[outer, 0] = growth
                remote(tbuf.at[outer, 0], tbuf.at[outer, 1], t_sem.at[0, outer], t_sem.at[1, outer], partner).start()
                set_along(growth, 0)
            tcur[0] = growth
            set_block(growth, 0)

        def far():
            remote(tbuf.at[outer, 0], tbuf.at[outer, 1], t_sem.at[0, outer], t_sem.at[1, outer], partner).wait_recv()
            tcur[1] = tbuf[outer, 1]
            set_block(tcur[1], 1)
            set_along(tcur[1], 1)

        pmine = hour_phi(chour[0], far)
        dest_col = to_row(jnp.sum(tcur[0] + tcur[1], axis=1, keepdims=True))
        send = pack_hour(pmine, dest_col)
        hmine[outer] = send
        start(hmine.at[outer], hbuf.at[outer], h_send.at[outer], h_recv.at[outer], cpeers, chip, 0)
        for g in range(2):
            set_whole(tcur[g], g)
        wait_bytes(hbuf.at[outer, pl.ds(0, nchip - 1)], h_recv.at[outer])
        s = add_up(hbuf.at[outer], range(nchip), send)
        dest_w = spread_group(s[:1], copies - 1) * (1.0 / (total_cols * nz))
        growth = (chour[0] * unpack_hour(s)) * ((1.0 / (total_rows * total_cols)) / dest_w)
        cbuf[outer, 0] = growth
        remote(cbuf.at[outer, 0], cbuf.at[outer, 1], c_sem.at[0, outer], c_sem.at[1, outer], partner).start()
        pmine = hour_phi_whole(growth)
        send = pack_tight(pmine)
        gmine[outer] = send
        start(gmine.at[outer], gbuf.at[outer], g_send.at[outer], g_recv.at[outer], everyone, chip, nchip)
        if outer == OUTER - 1:
            anchor_out[...] = uown[:, :rank]
            at = iota((piece, ncol), 1)
            at = (at // half + core) % 2 * half + at % half
            place = (at == me_orig * piece + iota((piece, ncol), 0)).astype(F32)
            d = jnp.concatenate(tcur, axis=1) / to_column(dest_w)
            dest_out[...] = lax.dot_general(place, d, (((1,), (1,)), ((), ())), precision=HIGH)
            wait_bytes(dbuf.at[pl.ds(0, norig - 1)], d_sem.at[0])
            acopy.wait_send()
            vcopy.wait_send()
            for e in range(OUTER * INNER * chunks):
                wait_bytes(ubuf.at[e, pl.ds(0, nx - 1)], u_send.at[e])
            for e in range(OUTER):
                wait_bytes(wbuf.at[e, pl.ds(0, nz - 1)], w_send.at[e])
                for k in range(2):
                    wait_bytes(zbuf.at[2 * e + k, pl.ds(0, nz - 1)], z_send.at[2 * e + k])
                wait_bytes(tbuf.at[e, 0], t_sem.at[0, e])
                wait_bytes(cbuf.at[e, 0], c_sem.at[0, e])
                wait_bytes(hbuf.at[e, pl.ds(0, nchip - 1)], h_send.at[e])
            for e in range(OUTER - 1):
                wait_bytes(gbuf.at[e, pl.ds(0, 2 * nchip - 1)], g_send.at[e])
        remote(cbuf.at[outer, 0], cbuf.at[outer, 1], c_sem.at[0, outer], c_sem.at[1, outer], partner).wait_recv()
        wait_bytes(gbuf.at[outer, pl.ds(0, 2 * nchip - 1)], g_recv.at[outer])
        chour = [
            c * (unpack_tight(add_up(gbuf.at[outer], range(q * nchip, (q + 1) * nchip), (send, None)[q]))
                 * (1.0 / (total_rows * total_cols)))
            for q, c in enumerate((growth, cbuf[outer, 1]))]
        w = jnp.sum(chour[0] + chour[1], axis=0, keepdims=True) * (1.0 / nhour)
        chour = [c / w for c in chour]
        hour = jnp.concatenate([jnp.where(core == k, chour[0], chour[1]) for k in range(2)], axis=0)
        if outer < OUTER - 1:
            set_hours(hour / dest_w)
            uown[...] = uown[...] * w
            ufar[...] = ufar[...] * w

    hi = hour.astype(BF16).astype(F32)
    mid = (hour - hi).astype(BF16).astype(F32)
    terms = jnp.where(group == 0, hi, jnp.where(group == 1, mid, jnp.where(group == 2, hour - hi - mid, 0.0)))
    hour_out[...] = lax.dot_general(
        diag_all.astype(BF16), terms.astype(BF16), (((1,), (1,)), ((), ())), preferred_element_type=F32)
    weight_out[...] = w[:, :rank]

    wait_bytes(gbuf.at[OUTER - 1, pl.ds(0, 2 * nchip - 1)], g_send.at[OUTER - 1])


def put_out(*refs):
    copies = [pltpu.make_async_copy(refs[q], refs[4 + q], refs[8].at[q]) for q in range(4)]
    for c in copies:
        c.start()
    for c in copies:
        c.wait()


def to_rows(row, rank):
    square = jnp.where(iota((rank, rank), 0) == iota((rank, rank), 1), jnp.broadcast_to(row, (rank, rank)), 0.0)
    return jnp.sum(square, axis=1, keepdims=True)


def on_device(counts, anchor_factor, dest_factor, hour_factor, weights):
    norig = lax.axis_size("orig")
    ndest = lax.axis_size("dest")
    nz, nx = norig // 2, 2 * ndest
    nchip = nz * ndest
    nrow, nhour, ncol = counts.shape
    rank = hour_factor.shape[1]
    khalf = nhour // 2
    chunks = nrow // 8
    hrow = -(-khalf // (8 * (LANES // rank - 1))) * 8
    prow = khalf * rank // LANES
    half = ncol // 2
    dma = pltpu.SemaphoreType.DMA
    vmem = pltpu.VMEM
    outs = pl.pallas_call(
        functools.partial(kernel, nz, ndest),
        out_shape=[
            jax.ShapeDtypeStruct(anchor_factor.shape, F32),
            jax.ShapeDtypeStruct(dest_factor.shape, F32),
            jax.ShapeDtypeStruct((rank, nhour), F32),
            jax.ShapeDtypeStruct((1, rank), F32),
        ],
        in_specs=[pl.BlockSpec(memory_space=pltpu.HBM)] * 5,
        out_specs=[pl.BlockSpec(memory_space=pltpu.VMEM)] * 4,
        scratch_shapes=[
            vmem((2, nrow, nhour, ncol), counts.dtype),
            vmem((chunks, 8 * nhour, ncol), F32),
            vmem((8 * nhour, LANES), F32),
            vmem((nrow, LANES), F32),
            vmem((nrow, LANES), F32),
            vmem((nhour, LANES), F32),
            vmem((2, LANES, half), BF16),
            vmem((2, 4 * rank, 2 * LANES), BF16),
            vmem((LANES, ncol), BF16),
            vmem((LANES, ncol), BF16),
            vmem((nrow * nhour, 2 * LANES), BF16),
            vmem((OUTER * INNER * chunks, 8, LANES), F32),
            vmem((OUTER * INNER * chunks, nx, 8, LANES), F32),
            vmem((OUTER, 8, LANES), F32),
            vmem((OUTER, nz, 8, LANES), F32),
            vmem((OUTER * 2, rank, LANES), F32),
            vmem((OUTER * 2, nz, rank, LANES), F32),
            vmem((OUTER, hrow, LANES), F32),
            vmem((OUTER, nchip, hrow, LANES), F32),
            vmem((OUTER, prow, LANES), F32),
            vmem((OUTER, 2 * nchip, prow, LANES), F32),
            vmem((2, nrow, LANES), F32),
            vmem((OUTER, 2, rank, LANES), F32),
            vmem((OUTER, 2, khalf, LANES), F32),
            vmem((norig,) + dest_factor.shape, F32),
            vmem(anchor_factor.shape, F32),
            vmem((rank, nhour), F32),
            vmem((1, rank), F32),
            dma((OUTER * INNER * chunks,)), dma((OUTER * INNER * chunks,)),
            dma((OUTER,)), dma((OUTER,)),
            dma((OUTER * 2,)), dma((OUTER * 2,)),
            dma((OUTER,)), dma((OUTER,)),
            dma((OUTER,)), dma((OUTER,)),
            dma((2, OUTER)), dma((2, OUTER)), dma((2,)), dma((2,)), dma((2,)), dma((4 + chunks,)),
        ],
        compiler_params=pltpu.CompilerParams(
            collective_id=0, has_side_effects=True, vmem_limit_bytes=67043328),
    )(counts, anchor_factor, dest_factor, hour_factor.T, weights.reshape(1, rank))
    outs = pl.pallas_call(
        put_out,
        out_shape=[jax.ShapeDtypeStruct(o.shape, F32) for o in outs],
        in_specs=[pl.BlockSpec(memory_space=pltpu.VMEM)] * 4,
        out_specs=[pl.BlockSpec(memory_space=pltpu.HBM)] * 4,
        scratch_shapes=[dma((4,))],
    )(*outs)
    return outs[0], outs[1], outs[2].T, outs[3].reshape(rank)


def solution(mesh):
    return jax.shard_map(
        on_device,
        mesh=mesh,
        in_specs=(P("orig", None, "dest"), P("orig", None), P(("dest", "orig"), None), P(), P()),
        out_specs=(P("orig", None), P(("dest", "orig"), None), P(), P()),
        check_vma=False,
    )
```
